256 devices in a mesh: width: 16 (over z, x_hi), chan: 16 (over y, x_lo, core).
Axes of the slice: x: 4 (x_hi: 2, x_lo: 2; x = x_hi * 2 + x_lo), y: 4, z: 8, core: 2. Of those that a mesh axis runs over, the one named last changes fastest.
Arguments:
- activations: bfloat16 [512, 2, 12288], P('chan', None, 'width'), may hold values from -6 to 6
- filters: bfloat16 [512, 3, 3, 512], P('chan'), may hold values from -0.125 to 0.125
- cotangent: bfloat16 [512, 2, 12288], P('chan', None, 'width'), may hold values from -6 to 6
Outputs:
- conv_output: bfloat16 [512, 2, 12288], P('chan', None, 'width')
- input_grad: bfloat16 [512, 2, 12288], P('chan', None, 'width')
- filter_grad: float32 [512, 3, 3, 512], P('chan')
The draws below stay inside these ranges and needn't reach their ends.
All inputs are finite; a program needn't handle non-finite values.
Results may differ from the reference program's by a relative error of at most 0.001.
Values may be sent and summed in bfloat16 or wider, within the bound.
A program may use at most 128 MiB of HBM per device.

```python
import math
import jax
import jax.numpy as jnp
from jax import lax

CIN = 512
COUT = 512
ROWS = 2
COLS = 12288


def spiked(entries, key, source, target, parts, factor):
    def block_of(dim):
        return (jnp.arange(entries.shape[dim]) // (entries.shape[dim] // parts)).reshape((-1,) + (1,) * (entries.ndim - 1 - dim))

    near = jax.random.permutation(key, parts)[block_of(target)]
    second = (block_of(target) + parts // 2) % parts
    return jnp.where((block_of(source) == near) | (block_of(source) == second), factor * entries, entries)


def block_levels(rng, shape, shards, least, top_value):
    loudness, own = 1.0, jax.random.fold_in(rng, 6)
    for dim, parts in shards:
        steps = jnp.exp(jax.random.uniform(jax.random.fold_in(own, dim), (parts,), jnp.float32, least / len(shards), top_value / len(shards)))
        loudness = loudness * jnp.repeat(steps, shape[dim] // parts).reshape([-1 if axis == dim else 1 for axis in range(len(shape))])
    return loudness


def gaussian(stream_key, extent, width, reach, shards=(), dtype=jnp.bfloat16):
    loudness = block_levels(stream_key, extent, shards, -0.22, 0.18) if shards else 1.0
    entries = jax.random.normal(stream_key, extent, jnp.float32) * width * loudness
    return jnp.minimum(jnp.maximum(entries, -reach), reach).astype(dtype)


def bell_draw_with(stream_key, extent, spread, bound, shards, heavy, kind=jnp.bfloat16):
    array = spread * jax.random.normal(stream_key, extent, jnp.float32)
    if shards:
        array = array * block_levels(stream_key, extent, shards, -0.22, 0.18)
    return jnp.clip(spiked(array, jax.random.fold_in(stream_key, 3), *heavy), -bound, bound).astype(kind)


def setup_inputs(seed: int = 0) -> dict:
    keys = jax.random.split(jax.random.key(seed), 4)
    activations = gaussian(keys[0], (CIN, ROWS, COLS), 1.0, 6.0, ((0, 16), (2, 16)))
    filters = bell_draw_with(keys[1], (CIN, 3, 3, COUT), (9 * CIN) ** -0.5, 0.125, ((0, 16),), (0, 3, 16, 2.0))
    cotangent = gaussian(keys[2], (COUT, ROWS, COLS), 1.0, 6.0, ((0, 16), (2, 16)))
    return {"activations": activations, "filters": filters, "cotangent": cotangent}


def tap_view(padded, tap_row, tap_col, rows, cols):
    return padded[:, tap_row:tap_row + rows, tap_col:tap_col + cols].reshape(padded.shape[0], rows * cols)

def reference(activations, filters, cotangent):
    rows = ROWS
    cols = COLS
    padded = jnp.pad(activations, ((0, 0), (1, 1), (1, 1)))
    grad_pad = jnp.pad(cotangent, ((0, 0), (1, 1), (1, 1)))
    flat_cot = cotangent.reshape(COUT, rows * cols)
    forward = jnp.zeros((COUT, rows * cols), jnp.float32)
    backward = jnp.zeros((CIN, rows * cols), jnp.float32)
    tap_grads = []
    for tap_row in range(3):
        for tap_col in range(3):
            kernel = filters[:, tap_row, tap_col, :]
            source = tap_view(padded, tap_row, tap_col, rows, cols)
            forward = forward + lax.dot_general(kernel, source, (((0,), (0,)), ((), ())), preferred_element_type=jnp.float32)
            backward = backward + jnp.dot(kernel, tap_view(grad_pad, 2 - tap_row, 2 - tap_col, rows, cols), preferred_element_type=jnp.float32)
            tap_grads.append(lax.dot_general(source, flat_cot, (((1,), (1,)), ((), ())), preferred_element_type=jnp.float32))
    factor = 1.0 / math.sqrt(rows * cols)
    filter_grad = jnp.stack(tap_grads, 1).reshape(CIN, 3, 3, COUT) * factor
    conv_output = forward.reshape(COUT, rows, cols).astype(jnp.bfloat16)
    input_grad = backward.reshape(CIN, rows, cols).astype(jnp.bfloat16)
    return (conv_output, input_grad, filter_grad)
```

```python
import math

import jax
import jax.numpy as jnp
from jax import lax
from jax.experimental import pallas as pl
from jax.experimental.pallas import tpu as pltpu
from jax.sharding import PartitionSpec as P

MESH = pl.DeviceIdType.MESH
BF16 = jnp.bfloat16
F32 = jnp.float32

Y_UP, Y_DOWN, ACROSS, CORE = "up", "down", "across", "core"


def arrived(piece, way):
    h, dy, dx, dc = piece
    if way == Y_UP:
        return (h, (dy - 1) % 4, dx, dc)
    if way == Y_DOWN:
        return (h, (dy + 1) % 4, dx, dc)
    if way == ACROSS:
        return (h, dy, 1 - dx, dc)
    return (h, dy, dx, 1 - dc)


def gather_plan(relay):
    first = [
        ((0, 0, 0, 0), Y_UP),
        ((0, 0, 0, 0), Y_DOWN),
        ((1, 0, 0, 0), ACROSS),
        ((1, 0, 0, 0), Y_UP),
        ((1, 0, 0, 0), Y_DOWN),
        ((0, 0, 0, 0), ACROSS),
        ((0, 0, 0, 0), CORE),
        ((1, 0, 0, 0), CORE),
    ]
    up = [Y_UP] if relay == Y_UP else []
    down = [Y_DOWN] if relay == Y_DOWN else []
    stages = [
        [(None, first)],
        [
            ((1, 0, 1, 0), [Y_UP, Y_DOWN, CORE]),
            ((0, 3, 0, 0), up + [ACROSS, CORE]),
            ((0, 1, 0, 0), down + [ACROSS, CORE]),
            ((1, 3, 0, 0), [Y_UP, CORE]),
            ((1, 1, 0, 0), [CORE]),
            ((0, 0, 1, 0), [CORE]),
        ],
        [
            ((1, 1, 1, 0), [Y_DOWN, CORE]),
            ((1, 3, 1, 0), [CORE]),
            ((0, 2, 0, 0), [ACROSS, CORE]),
            ((0, 3, 1, 0), [CORE]),
            ((0, 1, 1, 0), [CORE]),
            ((1, 2, 0, 0), [CORE]),
        ],
        [
            ((1, 2, 1, 0), [CORE]),
            ((0, 2, 1, 0), [CORE]),
        ],
    ]
    plan = []
    for stage in stages:
        steps = []
        for piece, sends in stage:
            if piece is not None:
                sends = [(piece, way) for way in sends]
            steps.append((piece, sends))
        plan.append(steps)
    return plan


def message_ids(plan):
    brings, number = {}, {}
    for steps in plan:
        for _, sends in steps:
            for piece, way in sends:
                number[(piece, way)] = len(number)
                brings[arrived(piece, way)] = number[(piece, way)]
    return brings, number


PLANS = [gather_plan(Y_UP), gather_plan(Y_DOWN)]
N_MSG = 30


def kernel(
    n_width,
    factor,
    x_ref,
    g_ref,
    f_ref,
    conv_ref,
    grad_ref,
    filt_ref,
    x_all,
    g_all,
    f_all,
    f_msg,
    halo,
    xs,
    part,
    rs_buf,
    e_out,
    e_in,
    y_buf,
    gat_send,
    gat_recv,
    f_send,
    f_recv,
    halo_send,
    halo_recv,
    rs_send,
    rs_recv,
    ag_send,
    ag_recv,
    e_send,
    e_recv,
):
    w = lax.axis_index("width")
    k = lax.axis_index("chan")
    py = k // 4
    px = (k // 2) % 2
    pc = k % 2
    cols = x_ref.shape[2]
    right = lax.rem(w + 1, n_width)
    left = lax.rem(w + n_width - 1, n_width)

    def chan_of(dy, dx, dc):
        y = lax.rem(py + dy, 4)
        x = 1 - px if dx else px
        c = 1 - pc if dc else pc
        return y * 4 + x * 2 + c

    ways = {
        Y_UP: chan_of(1, 0, 0),
        Y_DOWN: chan_of(3, 0, 0),
        ACROSS: chan_of(0, 1, 0),
        CORE: chan_of(0, 0, 1),
    }

    barrier = pltpu.get_barrier_semaphore()
    for d in range(1, 16):
        pl.semaphore_signal(
            barrier, inc=1, device_id={"chan": lax.rem(k + d, 16)}, device_id_type=MESH
        )
    for d in range(1, n_width):
        pl.semaphore_signal(
            barrier, inc=1, device_id={"width": lax.rem(w + d, n_width)}, device_id_type=MESH
        )

    lane = lax.broadcasted_iota(jnp.int32, (96, 128), 1)

    for tile in range(4):
        parts = [
            f_ref[:, b, :, tile * 128 : tile * 128 + 128].reshape(96, 128).astype(F32)
            for b in range(3)
        ]
        for j in range(4):
            out = jnp.zeros((96, 128), F32)
            for b in range(3):
                moved = parts[b]
                if (b - j) % 4:
                    moved = pltpu.roll(moved, ((b - j) % 4) * 32, 1)
                out = jnp.where(lane // 32 == b, moved, out)
            f_msg[tile * 4 + j] = out.astype(BF16).reshape(3, 32, 128)

    def own_rows(index):
        return pl.ds(pl.multiple_of(index * 32, 32), 32)

    x_all[:, own_rows(k), :] = x_ref[...]
    g_all[:, own_rows(k), :] = g_ref[...]
    f_all[:, own_rows(k), :] = f_msg[k]

    pl.semaphore_wait(barrier, 15 + n_width - 1)

    pending = []

    def start(copy):
        copy.start()
        pending.append(copy)

    arrays = [(g_all, g_ref), (x_all, x_ref)]
    brings_of = [message_ids(plan)[0] for plan in PLANS]
    number_of = [message_ids(plan)[1] for plan in PLANS]

    def piece_ref(which, piece):
        h, dy, dx, dc = piece
        return arrays[which][0].at[h, own_rows(chan_of(dy, dx, dc)), :]

    def gather_send(which, piece, way):
        m = number_of[which][(piece, way)]
        ref = piece_ref(which, piece)
        src = arrays[which][1].at[piece[0]] if piece[1:] == (0, 0, 0) else ref
        start(
            pltpu.make_async_remote_copy(
                src_ref=src,
                dst_ref=ref,
                send_sem=gat_send.at[which, m],
                recv_sem=gat_recv.at[which, m],
                device_id={"chan": ways[way]},
                device_id_type=MESH,
            )
        )

    def gather_wait(which, piece):
        m = brings_of[which][piece]
        ref = piece_ref(which, piece)
        pltpu.make_async_remote_copy(
            src_ref=ref,
            dst_ref=ref,
            send_sem=gat_send.at[which, m],
            recv_sem=gat_recv.at[which, m],
            device_id={"chan": ways[CORE]},
            device_id_type=MESH,
        ).wait_recv()

    def gather_stage(which, number):
        for piece, sends in PLANS[which][number]:
            if piece is not None:
                gather_wait(which, piece)
            for sent, way in sends:
                gather_send(which, sent, way)

    def gather_class(which, dy):
        for dx in range(2):
            for h in range(2):
                gather_wait(which, (h, dy, dx, 1))

    def halo_copy(side, device):
        src = x_ref.at[:, :, cols - 128 : cols] if side == 0 else x_ref.at[:, :, 0:128]
        return pltpu.make_async_remote_copy(
            src_ref=src,
            dst_ref=halo.at[side],
            send_sem=halo_send.at[side],
            recv_sem=halo_recv.at[side],
            device_id={"width": device},
            device_id_type=MESH,
        )

    halo_copies = [halo_copy(0, right), halo_copy(1, left)]
    for copy in halo_copies:
        start(copy)
    gather_stage(0, 0)

    lane64 = lax.broadcasted_iota(jnp.int32, (64, 128), 1)
    mine = x_ref[...].reshape(64, cols)
    xs[64:128, :] = mine
    mine = mine.astype(F32)
    xs[0:64, :] = pltpu.roll(mine, 1, 1).astype(BF16)
    xs[128:192, :] = pltpu.roll(mine, cols - 1, 1).astype(BF16)
    gather_stage(0, 1)
    for copy in halo_copies:
        copy.wait_recv()
    from_left = jnp.where(w > 0, pltpu.roll(halo[0].reshape(64, 128).astype(F32), 1, 1), 0.0)
    xs[0:64, 0:128] = jnp.where(lane64 == 0, from_left, xs[0:64, 0:128].astype(F32)).astype(BF16)
    from_right = jnp.where(
        w < n_width - 1, pltpu.roll(halo[1].reshape(64, 128).astype(F32), 127, 1), 0.0
    )
    xs[128:192, cols - 128 : cols] = jnp.where(
        lane64 == 127, from_right, xs[128:192, cols - 128 : cols].astype(F32)
    ).astype(BF16)

    def rs_copy(block, slot, device):
        return pltpu.make_async_remote_copy(
            src_ref=part.at[block % 4, :, pl.ds(pl.multiple_of(block // 4 * 8, 8), 8), :],
            dst_ref=rs_buf.at[slot],
            send_sem=rs_send.at[block],
            recv_sem=rs_recv.at[slot],
            device_id={"width": device},
            device_id_type=MESH,
        )

    def filter_class(dy):
        group = lax.rem(py + dy, 4)
        rows = pl.ds(pl.multiple_of(group * 128, 128), 128)
        taps = [
            lax.dot_general(
                xs[...], g_all[h, rows, :], (((1,), (1,)), ((), ())), preferred_element_type=F32
            )
            for h in range(2)
        ]
        for b in range(3):
            one, two = slice(b * 64, b * 64 + 32), slice(b * 64 + 32, b * 64 + 64)
            part[group, b] = taps[1][one]
            part[group, 3 + b] = taps[0][one] + taps[1][two]
            part[group, 6 + b] = taps[0][two]
        for c8 in range(4):
            block = c8 * 4 + group

            @pl.when(block != w)
            def _():
                rs_copy(block, w, block).start()

            @pl.when(block == w)
            def _():
                rs_buf[w] = part[group, :, c8 * 8 : c8 * 8 + 8, :]

    def f_copy(d):
        return pltpu.make_async_remote_copy(
            src_ref=f_msg.at[lax.rem(k + d, 16)],
            dst_ref=f_all.at[:, own_rows(k), :],
            send_sem=f_send.at[d],
            recv_sem=f_recv.at[d],
            device_id={"chan": lax.rem(k + d, 16)},
            device_id_type=MESH,
        )

    gather_class(0, 0)
    filter_class(0)
    gather_stage(1, 0)
    gather_stage(0, 2)
    gather_class(0, 3)
    filter_class(3)
    gather_class(0, 1)
    filter_class(1)
    gather_stage(0, 3)
    gather_stage(1, 1)
    for d in range(1, 16):
        start(f_copy(d))
    gather_class(0, 2)
    filter_class(2)
    gather_stage(1, 2)

    lane32 = lax.broadcasted_iota(jnp.int32, (32, cols), 1)

    def edge_copy(which, side, device):
        return pltpu.make_async_remote_copy(
            src_ref=e_out.at[which, side],
            dst_ref=e_in.at[which, side],
            send_sem=e_send.at[which, side],
            recv_sem=e_recv.at[which, side],
            device_id={"width": device},
            device_id_type=MESH,
        )

    def edges_out(which, taps):
        for h in range(2):
            e_out[which, 0, h] = taps[h][0][:, cols - 128 : cols]
            e_out[which, 1, h] = taps[h][2][:, 0:128]
        copies = [edge_copy(which, 0, right), edge_copy(which, 1, left)]
        for copy in copies:
            start(copy)
        for h in range(2):
            moved_right = jnp.where(lane32 == 0, 0.0, pltpu.roll(taps[h][0], 1, 1))
            moved_left = jnp.where(lane32 == cols - 1, 0.0, pltpu.roll(taps[h][2], cols - 1, 1))
            y_buf[which, h] = taps[h][1] + moved_right + moved_left
        return copies

    def edges_in(which, copies, out_ref):
        for copy in copies:
            copy.wait_recv()
        lane128 = lax.broadcasted_iota(jnp.int32, (32, 128), 1)
        for h in range(2):
            came = pltpu.roll(e_in[which, 0, h], 1, 1)
            y_buf[which, h, :, 0:128] += jnp.where((lane128 == 0) & (w > 0), came, 0.0)
            came = pltpu.roll(e_in[which, 1, h], 127, 1)
            y_buf[which, h, :, cols - 128 : cols] += jnp.where(
                (lane128 == 127) & (w < n_width - 1), came, 0.0
            )
            out_ref[h] = y_buf[which, h].astype(BF16)

    sums = None
    for h in range(2):
        block = f_ref[1 - h : 3 - h].reshape(192, f_ref.shape[3])
        term = jnp.dot(block, g_all[h], preferred_element_type=F32)
        sums = term if sums is None else sums + term
    taps = [[sums[h * 96 + b * 32 : h * 96 + b * 32 + 32] for b in (2, 1, 0)] for h in range(2)]
    grad_copies = edges_out(1, taps)

    gather_stage(1, 3)

    for d in range(1, n_width):
        source = lax.rem(w + d, n_width)
        rs_copy(source, source, source).wait_recv()
    total = rs_buf[0]
    for s in range(1, n_width):
        total = total + rs_buf[s]

    def block_ref(index):
        return filt_ref.at[
            :,
            pl.ds(pl.multiple_of(index // 4 * 8, 8), 8),
            pl.ds(pl.multiple_of(index % 4 * 128, 128), 128),
        ]

    filt_ref[
        :,
        pl.ds(pl.multiple_of(w // 4 * 8, 8), 8),
        pl.ds(pl.multiple_of(w % 4 * 128, 128), 128),
    ] = total * factor

    def ag_copy(index, d, device):
        return pltpu.make_async_remote_copy(
            src_ref=block_ref(index),
            dst_ref=block_ref(index),
            send_sem=ag_send.at[d],
            recv_sem=ag_recv.at[d],
            device_id={"width": device},
            device_id_type=MESH,
        )

    for d in range(1, n_width):
        start(ag_copy(w, d, lax.rem(w + d, n_width)))

    for which_dy in range(4):
        gather_class(1, which_dy)
    for d in range(1, 16):
        source = lax.rem(k + 16 - d, 16)
        pltpu.make_async_remote_copy(
            src_ref=f_msg.at[0],
            dst_ref=f_all.at[:, own_rows(source), :],
            send_sem=f_send.at[d],
            recv_sem=f_recv.at[d],
            device_id={"chan": source},
            device_id_type=MESH,
        ).wait_recv()
    depth = f_all.shape[1]
    field = x_all[...].reshape(2 * depth, cols)
    taps = []
    for h in range(2):
        block = f_all[1 - h : 3 - h].reshape(2 * depth, 128)
        sums = lax.dot_general(
            block, field, (((0,), (0,)), ((), ())), preferred_element_type=F32
        )
        taps.append([sums[b * 32 : b * 32 + 32] for b in range(3)])
    conv_copies = edges_out(0, taps)
    edges_in(1, grad_copies, grad_ref)
    edges_in(0, conv_copies, conv_ref)

    for d in range(1, n_width):
        source = lax.rem(w + n_width - d, n_width)
        ag_copy(source, d, source).wait_recv()
    for copy in pending:
        copy.wait_send()
    for d in range(1, n_width):
        block = lax.rem(w + d, n_width)
        rs_copy(block, w, block).wait_send()


def body(activations, filters, cotangent):
    cin_dev, rows, cols = activations.shape
    n_out = filters.shape[3]
    n_width = lax.axis_size("width")
    factor = 1.0 / math.sqrt(rows * cols * n_width)
    x = jnp.transpose(activations, (1, 0, 2))
    g = jnp.transpose(cotangent, (1, 0, 2))
    f = jnp.transpose(filters, (1, 2, 0, 3))
    vmem = pl.BlockSpec(memory_space=pltpu.VMEM)
    dma = pltpu.SemaphoreType.DMA

    def run(*refs):
        kernel(n_width, factor, *refs)

    conv, grad, filt = pl.pallas_call(
        run,
        out_shape=[
            jax.ShapeDtypeStruct((rows, cin_dev, cols), BF16),
            jax.ShapeDtypeStruct((rows, cin_dev, cols), BF16),
            jax.ShapeDtypeStruct((9, cin_dev, n_out), F32),
        ],
        in_specs=[vmem] * 3,
        out_specs=[vmem] * 3,
        scratch_shapes=[
            pltpu.VMEM((rows, n_out, cols), BF16),
            pltpu.VMEM((rows, n_out, cols), BF16),
            pltpu.VMEM((3, n_out, 128), BF16),
            pltpu.VMEM((16, 3, cin_dev, 128), BF16),
            pltpu.VMEM((2, rows, cin_dev, 128), BF16),
            pltpu.VMEM((192, cols), BF16),
            pltpu.VMEM((4, 9, cin_dev, 128), F32),
            pltpu.VMEM((n_width, 9, 8, 128), F32),
            pltpu.VMEM((2, 2, rows, cin_dev, 128), F32),
            pltpu.VMEM((2, 2, rows, cin_dev, 128), F32),
            pltpu.VMEM((2, rows, cin_dev, cols), F32),
            dma((2, N_MSG)),
            dma((2, N_MSG)),
            dma((16,)),
            dma((16,)),
            dma((2,)),
            dma((2,)),
            dma((n_width,)),
            dma((n_width,)),
            dma((n_width,)),
            dma((n_width,)),
            dma((2, 2)),
            dma((2, 2)),
        ],
        compiler_params=pltpu.CompilerParams(
            collective_id=0, has_side_effects=True, vmem_limit_bytes=40 * 1024 * 1024
        ),
        name="conv_all",
    )(x, g, f)
    conv = jnp.transpose(conv, (1, 0, 2))
    grad = jnp.transpose(grad, (1, 0, 2))
    filt = jnp.transpose(filt.reshape(3, 3, cin_dev, n_out), (2, 0, 1, 3))
    return conv, grad, filt


def solution(mesh):
    in_specs = (P("chan", None, "width"), P("chan", None, None, None), P("chan", None, "width"))
    out_specs = (P("chan", None, "width"), P("chan", None, "width"), P("chan", None, None, None))
    return jax.shard_map(body, mesh=mesh, in_specs=in_specs, out_specs=out_specs, check_vma=False)
```

```python
import math

import jax
import jax.numpy as jnp
from jax import lax
from jax.experimental import pallas as pl
from jax.experimental.pallas import tpu as pltpu
from jax.sharding import PartitionSpec as P

MESH = pl.DeviceIdType.MESH
BF16 = jnp.bfloat16
F32 = jnp.float32

Y_ONE, Y_TWO, Y_THREE, ACROSS, CORE = (1, 0, 0), (2, 0, 0), (3, 0, 0), (0, 1, 0), (0, 0, 1)
ALONG = [Y_ONE, Y_THREE, Y_TWO]


def arrived(piece, way):
    h, dy, dx, dc = piece
    return (h, (dy - way[0]) % 4, (dx + way[1]) % 2, (dc + way[2]) % 2)


OWN = (0, 0, 0)
STAGES = [
    [
        ((1,) + OWN, [ACROSS]),
        ((0,) + OWN, [ACROSS] + ALONG),
        ((1,) + OWN, ALONG),
        ((0,) + OWN, [CORE]),
        ((1,) + OWN, [CORE]),
    ],
    [
        ((1, 0, 1, 0), ALONG + [CORE]),
        ((0, 0, 1, 0), [CORE]),
    ],
    [
        ((0, 1, 0, 0), [ACROSS, CORE]),
        ((0, 3, 0, 0), [ACROSS, CORE]),
        ((0, 2, 0, 0), [ACROSS, CORE]),
        ((1, 1, 0, 0), [CORE]),
        ((1, 3, 0, 0), [CORE]),
        ((1, 2, 0, 0), [CORE]),
    ],
    [
        ((1, 1, 1, 0), [CORE]),
        ((1, 3, 1, 0), [CORE]),
        ((0, 1, 1, 0), [CORE]),
        ((0, 3, 1, 0), [CORE]),
    ],
    [
        ((1, 2, 1, 0), [CORE]),
        ((0, 2, 1, 0), [CORE]),
    ],
]

STAGES_X = [
    [
        ((1,) + OWN, [ACROSS]),
        ((0,) + OWN, [ACROSS]),
        ((1,) + OWN, ALONG),
        ((0,) + OWN, ALONG),
        ((0,) + OWN, [CORE]),
        ((1,) + OWN, [CORE]),
    ],
    [
        ((1, 0, 1, 0), ALONG + [CORE]),
        ((0, 0, 1, 0), ALONG + [CORE]),
    ],
    [
        ((1, 1, 0, 0), [CORE]),
        ((1, 3, 0, 0), [CORE]),
        ((0, 1, 0, 0), [CORE]),
        ((0, 3, 0, 0), [CORE]),
        ((1, 2, 0, 0), [CORE]),
        ((0, 2, 0, 0), [CORE]),
    ],
    [
        ((1, 1, 1, 0), [CORE]),
        ((1, 3, 1, 0), [CORE]),
        ((0, 1, 1, 0), [CORE]),
        ((0, 3, 1, 0), [CORE]),
    ],
    [
        ((1, 2, 1, 0), [CORE]),
        ((0, 2, 1, 0), [CORE]),
    ],
]


def message_ids(stages):
    number, brings = {}, {}
    for steps in stages:
        for piece, ways in steps:
            for way in ways:
                number[(piece, way)] = len(number)
                brings[arrived(piece, way)] = number[(piece, way)]
    return number, brings


PLANS = [STAGES, STAGES_X]
IDS = [message_ids(stages) for stages in PLANS]
N_MSG = 32
Z_ORDER = [1, 7, 2, 6, 3, 5, 4]


def kernel(
    n_width,
    factor,
    x_ref,
    g_ref,
    f_ref,
    conv_ref,
    grad_ref,
    filt_ref,
    x_all,
    g_all,
    f_all,
    f_msg,
    halo,
    xs,
    part,
    pair_out,
    pair_in,
    rs_buf,
    blocks,
    e_out,
    e_in,
    y_buf,
    gat_send,
    gat_recv,
    f_send,
    f_recv,
    halo_send,
    halo_recv,
    pair_send,
    pair_recv,
    rs_send,
    rs_recv,
    ag_send,
    ag_recv,
    e_send,
    e_recv,
):
    w = lax.axis_index("width")
    k = lax.axis_index("chan")
    py = k // 4
    px = (k // 2) % 2
    pc = k % 2
    cols = x_ref.shape[2]
    n_z = n_width // 2
    z = w // 2
    column = w % 2
    across = w + 1 - 2 * column
    right = lax.rem(w + 1, n_width)
    left = lax.rem(w + n_width - 1, n_width)

    def chan_of(dy, dx, dc):
        y = lax.rem(py + dy, 4)
        x = 1 - px if dx else px
        c = 1 - pc if dc else pc
        return y * 4 + x * 2 + c

    barrier = pltpu.get_barrier_semaphore()
    for d in range(1, 16):
        pl.semaphore_signal(
            barrier, inc=1, device_id={"chan": lax.rem(k + d, 16)}, device_id_type=MESH
        )
    near_width = [lax.rem(w + 2 * d, n_width) for d in range(1, n_z)] + [right, left]
    for device in near_width:
        pl.semaphore_signal(barrier, inc=1, device_id={"width": device}, device_id_type=MESH)

    lane = lax.broadcasted_iota(jnp.int32, (96, 128), 1)

    for tile in range(4):
        parts = [
            f_ref[:, b, :, tile * 128 : tile * 128 + 128].reshape(96, 128).astype(F32)
            for b in range(3)
        ]
        for j in range(4):
            out = jnp.zeros((96, 128), F32)
            for b in range(3):
                moved = parts[b]
                if (b - j) % 4:
                    moved = pltpu.roll(moved, ((b - j) % 4) * 32, 1)
                out = jnp.where(lane // 32 == b, moved, out)
            f_msg[tile * 4 + j] = out.astype(BF16).reshape(3, 32, 128)

    def own_rows(index):
        return pl.ds(pl.multiple_of(index * 32, 32), 32)

    x_all[:, own_rows(k), :] = x_ref[...]
    g_all[:, own_rows(k), :] = g_ref[...]
    f_all[:, own_rows(k), :] = f_msg[k]

    pl.semaphore_wait(barrier, 15 + len(near_width))

    pending = []

    def start(copy):
        copy.start()
        pending.append(copy)

    arrays = [(g_all, g_ref), (x_all, x_ref)]

    def piece_ref(which, piece):
        h, dy, dx, dc = piece
        return arrays[which][0].at[h, own_rows(chan_of(dy, dx, dc)), :]

    def gather_send(which, piece, way):
        m = IDS[which][0][(piece, way)]
        ref = piece_ref(which, piece)
        src = arrays[which][1].at[piece[0]] if piece[1:] == OWN else ref
        start(
            pltpu.make_async_remote_copy(
                src_ref=src,
                dst_ref=ref,
                send_sem=gat_send.at[which, m],
                recv_sem=gat_recv.at[which, m],
                device_id={"chan": chan_of(*way)},
                device_id_type=MESH,
            )
        )

    def gather_wait(which, piece):
        m = IDS[which][1][piece]
        ref = piece_ref(which, piece)
        pltpu.make_async_remote_copy(
            src_ref=ref,
            dst_ref=ref,
            send_sem=gat_send.at[which, m],
            recv_sem=gat_recv.at[which, m],
            device_id={"chan": chan_of(*CORE)},
            device_id_type=MESH,
        ).wait_recv()

    def gather_stage(which, number):
        for piece, ways in PLANS[which][number]:
            if piece[1:] != OWN:
                gather_wait(which, piece)
            for way in ways:
                gather_send(which, piece, way)

    def gather_class(which, dy):
        for dx in range(2):
            for h in range(2):
                gather_wait(which, (h, dy, dx, 1))

    def halo_copy(side, device):
        src = x_ref.at[:, :, cols - 128 : cols] if side == 0 else x_ref.at[:, :, 0:128]
        return pltpu.make_async_remote_copy(
            src_ref=src,
            dst_ref=halo.at[side],
            send_sem=halo_send.at[side],
            recv_sem=halo_recv.at[side],
            device_id={"width": device},
            device_id_type=MESH,
        )

    halo_copies = [halo_copy(0, right), halo_copy(1, left)]
    for copy in halo_copies:
        start(copy)
    gather_stage(0, 0)

    lane64 = lax.broadcasted_iota(jnp.int32, (64, 128), 1)
    mine = x_ref[...].reshape(64, cols)
    xs[64:128, :] = mine
    mine = mine.astype(F32)
    xs[0:64, :] = pltpu.roll(mine, 1, 1).astype(BF16)
    xs[128:192, :] = pltpu.roll(mine, cols - 1, 1).astype(BF16)
    gather_stage(0, 1)
    for copy in halo_copies:
        copy.wait_recv()
    from_left = jnp.where(w > 0, pltpu.roll(halo[0].reshape(64, 128).astype(F32), 1, 1), 0.0)
    xs[0:64, 0:128] = jnp.where(lane64 == 0, from_left, xs[0:64, 0:128].astype(F32)).astype(BF16)
    from_right = jnp.where(
        w < n_width - 1, pltpu.roll(halo[1].reshape(64, 128).astype(F32), 127, 1), 0.0
    )
    xs[128:192, cols - 128 : cols] = jnp.where(
        lane64 == 127, from_right, xs[128:192, cols - 128 : cols].astype(F32)
    ).astype(BF16)

    def group_of(dy):
        return lax.rem(py + dy, 4)

    def rs_copy(dy, d):
        return pltpu.make_async_remote_copy(
            src_ref=part.at[group_of(dy), pl.ds(2 * lax.rem(z + d, n_z), 2)],
            dst_ref=rs_buf.at[d, group_of(dy)],
            send_sem=rs_send.at[dy, d],
            recv_sem=rs_recv.at[dy, d],
            device_id={"width": lax.rem(w + 2 * d, n_width)},
            device_id_type=MESH,
        )

    def pair_copy(dy):
        return pltpu.make_async_remote_copy(
            src_ref=pair_out.at[dy],
            dst_ref=pair_in.at[dy],
            send_sem=pair_send.at[dy],
            recv_sem=pair_recv.at[dy],
            device_id={"width": across},
            device_id_type=MESH,
        )

    def ag_copy(dy, index, slot, device):
        ref = blocks.at[group_of(dy), index]
        return pltpu.make_async_remote_copy(
            src_ref=ref,
            dst_ref=ref,
            send_sem=ag_send.at[dy, slot],
            recv_sem=ag_recv.at[dy, slot],
            device_id={"width": device},
            device_id_type=MESH,
        )

    def filter_class(dy):
        group = group_of(dy)
        rows = pl.ds(pl.multiple_of(group * 128, 128), 128)
        taps = [
            lax.dot_general(
                xs[...], g_all[h, rows, :], (((1,), (1,)), ((), ())), preferred_element_type=F32
            )
            for h in range(2)
        ]
        for b in range(3):
            one, two = slice(b * 64, b * 64 + 32), slice(b * 64 + 32, b * 64 + 64)
            three = [taps[1][one], taps[0][one] + taps[1][two], taps[0][two]]
            for a in range(3):
                part[group, :, a * 3 + b] = three[a].reshape(n_width, 2, 128)
        for d in Z_ORDER:
            start(rs_copy(dy, d))

    def sum_along_z(dy):
        group = group_of(dy)
        for d in Z_ORDER:
            rs_copy(dy, d).wait_recv()
        for side in range(2):
            total = part[group, 2 * z + side]
            for d in range(1, n_z):
                total = total + rs_buf[d, group, side]
            part[group, 2 * z + side] = total
        pair_out[dy] = part[group, across]
        start(pair_copy(dy))

    def hand_out(dy):
        group = group_of(dy)
        pair_copy(dy).wait_recv()
        blocks[group, w] = (part[group, w] + pair_in[dy]) * factor
        for d in Z_ORDER:
            start(ag_copy(dy, w, d, lax.rem(w + 2 * d, n_width)))
        start(ag_copy(dy, w, n_z, across))

    def relay(dy):
        for d in Z_ORDER:
            source = lax.rem(w + n_width - 2 * d, n_width)
            ag_copy(dy, source, d, across).wait_recv()
            start(ag_copy(dy, source, n_z + d, across))

    def f_copy(d):
        return pltpu.make_async_remote_copy(
            src_ref=f_msg.at[lax.rem(k + d, 16)],
            dst_ref=f_all.at[:, own_rows(k), :],
            send_sem=f_send.at[d],
            recv_sem=f_recv.at[d],
            device_id={"chan": lax.rem(k + d, 16)},
            device_id_type=MESH,
        )

    gather_class(0, 0)
    filter_class(0)
    gather_stage(0, 2)
    gather_stage(0, 3)
    gather_class(0, 1)
    filter_class(1)
    gather_class(0, 3)
    filter_class(3)
    gather_stage(0, 4)
    gather_class(0, 2)
    filter_class(2)
    gather_stage(1, 0)
    sum_along_z(0)
    gather_stage(1, 1)
    for d in range(1, 16):
        start(f_copy(d))
    sum_along_z(1)
    hand_out(0)
    sum_along_z(3)
    hand_out(1)
    gather_stage(1, 2)

    lane32 = lax.broadcasted_iota(jnp.int32, (32, cols), 1)

    def edge_copy(which, side, device):
        return pltpu.make_async_remote_copy(
            src_ref=e_out.at[which, side],
            dst_ref=e_in.at[which, side],
            send_sem=e_send.at[which, side],
            recv_sem=e_recv.at[which, side],
            device_id={"width": device},
            device_id_type=MESH,
        )

    def edges_out(which, taps):
        for h in range(2):
            e_out[which, 0, h] = taps[h][0][:, cols - 128 : cols]
            e_out[which, 1, h] = taps[h][2][:, 0:128]
        copies = [edge_copy(which, 0, right), edge_copy(which, 1, left)]
        for copy in copies:
            start(copy)
        for h in range(2):
            moved_right = jnp.where(lane32 == 0, 0.0, pltpu.roll(taps[h][0], 1, 1))
            moved_left = jnp.where(lane32 == cols - 1, 0.0, pltpu.roll(taps[h][2], cols - 1, 1))
            y_buf[which, h] = taps[h][1] + moved_right + moved_left
        return copies

    def edges_in(which, copies, out_ref):
        for copy in copies:
            copy.wait_recv()
        lane128 = lax.broadcasted_iota(jnp.int32, (32, 128), 1)
        for h in range(2):
            came = pltpu.roll(e_in[which, 0, h], 1, 1)
            y_buf[which, h, :, 0:128] += jnp.where((lane128 == 0) & (w > 0), came, 0.0)
            came = pltpu.roll(e_in[which, 1, h], 127, 1)
            y_buf[which, h, :, cols - 128 : cols] += jnp.where(
                (lane128 == 127) & (w < n_width - 1), came, 0.0
            )
            out_ref[h] = y_buf[which, h].astype(BF16)

    sums = None
    for h in range(2):
        block = f_ref[1 - h : 3 - h].reshape(192, f_ref.shape[3])
        term = jnp.dot(block, g_all[h], preferred_element_type=F32)
        sums = term if sums is None else sums + term
    taps = [[sums[h * 96 + b * 32 : h * 96 + b * 32 + 32] for b in (2, 1, 0)] for h in range(2)]
    grad_copies = edges_out(1, taps)

    sum_along_z(2)
    hand_out(3)
    gather_stage(1, 3)
    gather_stage(1, 4)
    hand_out(2)
    relay(0)
    relay(1)
    relay(3)

    for which_dy in range(4):
        gather_class(1, which_dy)
    for d in range(1, 16):
        source = lax.rem(k + 16 - d, 16)
        pltpu.make_async_remote_copy(
            src_ref=f_msg.at[0],
            dst_ref=f_all.at[:, own_rows(source), :],
            send_sem=f_send.at[d],
            recv_sem=f_recv.at[d],
            device_id={"chan": source},
            device_id_type=MESH,
        ).wait_recv()
    depth = f_all.shape[1]
    field = x_all[...].reshape(2 * depth, cols)
    taps = []
    for h in range(2):
        block = f_all[1 - h : 3 - h].reshape(2 * depth, 128)
        sums = lax.dot_general(
            block, field, (((0,), (0,)), ((), ())), preferred_element_type=F32
        )
        taps.append([sums[b * 32 : b * 32 + 32] for b in range(3)])
    conv_copies = edges_out(0, taps)
    relay(2)
    edges_in(1, grad_copies, grad_ref)
    edges_in(0, conv_copies, conv_ref)

    for dy in (0, 1, 3, 2):
        for d in range(n_z):
            source = lax.rem(across + n_width - 2 * d, n_width)
            ag_copy(dy, source, n_z + d, across).wait_recv()
    for group in range(4):
        for tap in range(9):
            filt_ref[tap, :, group * 128 : group * 128 + 128] = blocks[group, :, tap].reshape(
                2 * n_width, 128
            )
    for copy in pending:
        copy.wait_send()


def body(activations, filters, cotangent):
    cin_dev, rows, cols = activations.shape
    n_out = filters.shape[3]
    n_width = lax.axis_size("width")
    factor = 1.0 / math.sqrt(rows * cols * n_width)
    x = jnp.transpose(activations, (1, 0, 2))
    g = jnp.transpose(cotangent, (1, 0, 2))
    f = jnp.transpose(filters, (1, 2, 0, 3))
    vmem = pl.BlockSpec(memory_space=pltpu.VMEM)
    dma = pltpu.SemaphoreType.DMA

    def run(*refs):
        kernel(n_width, factor, *refs)

    conv, grad, filt = pl.pallas_call(
        run,
        out_shape=[
            jax.ShapeDtypeStruct((rows, cin_dev, cols), BF16),
            jax.ShapeDtypeStruct((rows, cin_dev, cols), BF16),
            jax.ShapeDtypeStruct((9, cin_dev, n_out), F32),
        ],
        in_specs=[vmem] * 3,
        out_specs=[vmem] * 3,
        scratch_shapes=[
            pltpu.VMEM((rows, n_out, cols), BF16),
            pltpu.VMEM((rows, n_out, cols), BF16),
            pltpu.VMEM((3, n_out, 128), BF16),
            pltpu.VMEM((16, 3, cin_dev, 128), BF16),
            pltpu.VMEM((2, rows, cin_dev, 128), BF16),
            pltpu.VMEM((192, cols), BF16),
            pltpu.VMEM((4, n_width, 9, 2, 128), F32),
            pltpu.VMEM((4, 9, 2, 128), F32),
            pltpu.VMEM((4, 9, 2, 128), F32),
            pltpu.VMEM((n_width // 2, 4, 2, 9, 2, 128), F32),
            pltpu.VMEM((4, n_width, 9, 2, 128), F32),
            pltpu.VMEM((2, 2, rows, cin_dev, 128), F32),
            pltpu.VMEM((2, 2, rows, cin_dev, 128), F32),
            pltpu.VMEM((2, rows, cin_dev, cols), F32),
            dma((2, N_MSG)),
            dma((2, N_MSG)),
            dma((16,)),
            dma((16,)),
            dma((2,)),
            dma((2,)),
            dma((4,)),
            dma((4,)),
            dma((4, n_width // 2)),
            dma((4, n_width // 2)),
            dma((4, n_width)),
            dma((4, n_width)),
            dma((2, 2)),
            dma((2, 2)),
        ],
        compiler_params=pltpu.CompilerParams(
            collective_id=0, has_side_effects=True, vmem_limit_bytes=40 * 1024 * 1024
        ),
        name="conv_all",
    )(x, g, f)
    conv = jnp.transpose(conv, (1, 0, 2))
    grad = jnp.transpose(grad, (1, 0, 2))
    filt = jnp.transpose(filt.reshape(3, 3, cin_dev, n_out), (2, 0, 1, 3))
    return conv, grad, filt


def solution(mesh):
    in_specs = (P("chan", None, "width"), P("chan", None, None, None), P("chan", None, "width"))
    out_specs = (P("chan", None, "width"), P("chan", None, "width"), P("chan", None, None, None))
    return jax.shard_map(body, mesh=mesh, in_specs=in_specs, out_specs=out_specs, check_vma=False)
```

```python
import math

import jax
import jax.numpy as jnp
from jax import lax
from jax.experimental import pallas as pl
from jax.experimental.pallas import tpu as pltpu
from jax.sharding import PartitionSpec as P

MESH = pl.DeviceIdType.MESH
BF16 = jnp.bfloat16
F32 = jnp.float32

Y_ONE, Y_TWO, Y_THREE, ACROSS, CORE = (1, 0, 0), (2, 0, 0), (3, 0, 0), (0, 1, 0), (0, 0, 1)
ALONG = [Y_ONE, Y_THREE, Y_TWO]


def arrived(piece, way):
    h, dy, dx, dc = piece
    return (h, (dy - way[0]) % 4, (dx + way[1]) % 2, (dc + way[2]) % 2)


OWN = (0, 0, 0)
STAGES = [
    [
        ((1,) + OWN, [ACROSS]),
        ((0,) + OWN, [ACROSS] + ALONG),
        ((1,) + OWN, ALONG),
        ((0,) + OWN, [CORE]),
        ((1,) + OWN, [CORE]),
    ],
    [
        ((1, 0, 1, 0), ALONG + [CORE]),
        ((0, 0, 1, 0), [CORE]),
    ],
    [
        ((0, 1, 0, 0), [ACROSS, CORE]),
        ((0, 3, 0, 0), [ACROSS, CORE]),
        ((0, 2, 0, 0), [ACROSS, CORE]),
        ((1, 1, 0, 0), [CORE]),
        ((1, 3, 0, 0), [CORE]),
        ((1, 2, 0, 0), [CORE]),
    ],
    [
        ((1, 1, 1, 0), [CORE]),
        ((1, 3, 1, 0), [CORE]),
        ((0, 1, 1, 0), [CORE]),
        ((0, 3, 1, 0), [CORE]),
    ],
    [
        ((1, 2, 1, 0), [CORE]),
        ((0, 2, 1, 0), [CORE]),
    ],
]

STAGES_X = [
    [
        ((1,) + OWN, [ACROSS]),
        ((0,) + OWN, [ACROSS]),
        ((1,) + OWN, ALONG),
        ((0,) + OWN, ALONG),
        ((0,) + OWN, [CORE]),
        ((1,) + OWN, [CORE]),
    ],
    [
        ((1, 0, 1, 0), ALONG + [CORE]),
        ((0, 0, 1, 0), ALONG + [CORE]),
    ],
    [
        ((1, 1, 0, 0), [CORE]),
        ((1, 3, 0, 0), [CORE]),
        ((0, 1, 0, 0), [CORE]),
        ((0, 3, 0, 0), [CORE]),
        ((1, 2, 0, 0), [CORE]),
        ((0, 2, 0, 0), [CORE]),
    ],
    [
        ((1, 1, 1, 0), [CORE]),
        ((1, 3, 1, 0), [CORE]),
        ((0, 1, 1, 0), [CORE]),
        ((0, 3, 1, 0), [CORE]),
    ],
    [
        ((1, 2, 1, 0), [CORE]),
        ((0, 2, 1, 0), [CORE]),
    ],
]


def message_ids(stages):
    number, brings = {}, {}
    for steps in stages:
        for piece, ways in steps:
            for way in ways:
                number[(piece, way)] = len(number)
                brings[arrived(piece, way)] = number[(piece, way)]
    return number, brings


PLANS = [STAGES, STAGES_X]
IDS = [message_ids(stages) for stages in PLANS]
N_MSG = 32
Z_ORDER = [1, 7, 2, 6, 3, 5, 4]
BOTH = (2,)


def kernel(
    n_width,
    factor,
    x_ref,
    g_ref,
    f_ref,
    conv_ref,
    grad_ref,
    blocks,
    x_all,
    g_all,
    f_all,
    f_msg,
    halo,
    xs,
    part,
    pair_in,
    rs_buf,
    e_out,
    e_in,
    y_buf,
    gat_send,
    gat_recv,
    f_send,
    f_recv,
    halo_send,
    halo_recv,
    pair_send,
    pair_recv,
    rs_send,
    rs_recv,
    ag_send,
    ag_recv,
    e_send,
    e_recv,
):
    w = lax.axis_index("width")
    k = lax.axis_index("chan")
    py = k // 4
    px = (k // 2) % 2
    pc = k % 2
    cols = x_ref.shape[2]
    n_z = n_width // 2
    z = w // 2
    column = w % 2
    across = w + 1 - 2 * column
    right = lax.rem(w + 1, n_width)
    left = lax.rem(w + n_width - 1, n_width)

    def chan_of(dy, dx, dc):
        y = lax.rem(py + dy, 4)
        x = 1 - px if dx else px
        c = 1 - pc if dc else pc
        return y * 4 + x * 2 + c

    barrier = pltpu.get_barrier_semaphore()
    for d in range(1, 16):
        pl.semaphore_signal(
            barrier, inc=1, device_id={"chan": lax.rem(k + d, 16)}, device_id_type=MESH
        )
    near_width = [lax.rem(w + 2 * d, n_width) for d in range(1, n_z)] + [right, left]
    for device in near_width:
        pl.semaphore_signal(barrier, inc=1, device_id={"width": device}, device_id_type=MESH)

    def own_rows(index):
        return pl.ds(pl.multiple_of(index * 32, 32), 32)

    pl.semaphore_wait(barrier, 15 + len(near_width))

    pending = []

    def start(copy):
        copy.start()
        pending.append(copy)

    arrays = [(g_all, g_ref), (x_all, x_ref)]

    def piece_ref(which, piece):
        h, dy, dx, dc = piece
        return arrays[which][0].at[h, own_rows(chan_of(dy, dx, dc)), :]

    def gather_send(which, piece, way):
        m = IDS[which][0][(piece, way)]
        ref = piece_ref(which, piece)
        src = arrays[which][1].at[piece[0]] if piece[1:] == OWN else ref
        start(
            pltpu.make_async_remote_copy(
                src_ref=src,
                dst_ref=ref,
                send_sem=gat_send.at[which, m],
                recv_sem=gat_recv.at[which, m],
                device_id={"chan": chan_of(*way)},
                device_id_type=MESH,
            )
        )

    def gather_wait(which, piece):
        m = IDS[which][1][piece]
        ref = piece_ref(which, piece)
        pltpu.make_async_remote_copy(
            src_ref=ref,
            dst_ref=ref,
            send_sem=gat_send.at[which, m],
            recv_sem=gat_recv.at[which, m],
            device_id={"chan": chan_of(*CORE)},
            device_id_type=MESH,
        ).wait_recv()

    def gather_stage(which, number):
        for piece, ways in PLANS[which][number]:
            if piece[1:] != OWN:
                gather_wait(which, piece)
            for way in ways:
                gather_send(which, piece, way)

    def gather_class(which, dy):
        for dx in range(2):
            for h in range(2):
                gather_wait(which, (h, dy, dx, 1))

    def halo_copy(side, device):
        src = x_ref.at[:, :, cols - 128 : cols] if side == 0 else x_ref.at[:, :, 0:128]
        return pltpu.make_async_remote_copy(
            src_ref=src,
            dst_ref=halo.at[side],
            send_sem=halo_send.at[side],
            recv_sem=halo_recv.at[side],
            device_id={"width": device},
            device_id_type=MESH,
        )

    halo_copies = [halo_copy(0, right), halo_copy(1, left)]
    gather_stage(0, 0)
    for copy in halo_copies:
        start(copy)

    x_all[:, own_rows(k), :] = x_ref[...]
    g_all[:, own_rows(k), :] = g_ref[...]

    lane64 = lax.broadcasted_iota(jnp.int32, (64, 128), 1)
    mine = x_ref[...].reshape(64, cols)
    xs[64:128, :] = mine
    mine = mine.astype(F32)
    xs[0:64, :] = pltpu.roll(mine, 1, 1).astype(BF16)
    xs[128:192, :] = pltpu.roll(mine, cols - 1, 1).astype(BF16)
    gather_stage(0, 1)
    for copy in halo_copies:
        copy.wait_recv()
    from_left = jnp.where(w > 0, pltpu.roll(halo[0].reshape(64, 128).astype(F32), 1, 1), 0.0)
    xs[0:64, 0:128] = jnp.where(lane64 == 0, from_left, xs[0:64, 0:128].astype(F32)).astype(BF16)
    from_right = jnp.where(
        w < n_width - 1, pltpu.roll(halo[1].reshape(64, 128).astype(F32), 127, 1), 0.0
    )
    xs[128:192, cols - 128 : cols] = jnp.where(
        lane64 == 127, from_right, xs[128:192, cols - 128 : cols].astype(F32)
    ).astype(BF16)

    def group_of(dy):
        return lax.rem(py + dy, 4)

    def rs_copy(dy, d):
        return pltpu.make_async_remote_copy(
            src_ref=part.at[group_of(dy), pl.ds(2 * lax.rem(z + d, n_z), 2)],
            dst_ref=rs_buf.at[d, group_of(dy)],
            send_sem=rs_send.at[dy, d],
            recv_sem=rs_recv.at[dy, d],
            device_id={"width": lax.rem(w + 2 * d, n_width)},
            device_id_type=MESH,
        )

    def pair_copy(dy):
        return pltpu.make_async_remote_copy(
            src_ref=part.at[group_of(dy), pl.ds(2 * z, 2) if dy in BOTH else pl.ds(across, 1)],
            dst_ref=pair_in.at[dy, pl.ds(0, 2 if dy in BOTH else 1)],
            send_sem=pair_send.at[dy],
            recv_sem=pair_recv.at[dy],
            device_id={"width": across},
            device_id_type=MESH,
        )

    def ag_copy(dy, index, slot, device):
        owners = pl.ds(2 * (index // 2), 2) if dy in BOTH else pl.ds(index, 1)
        ref = blocks.at[group_of(dy), owners]
        return pltpu.make_async_remote_copy(
            src_ref=ref,
            dst_ref=ref,
            send_sem=ag_send.at[dy, slot],
            recv_sem=ag_recv.at[dy, slot],
            device_id={"width": device},
            device_id_type=MESH,
        )

    def filter_class(dy):
        group = group_of(dy)
        rows = pl.ds(pl.multiple_of(group * 128, 128), 128)
        taps = [
            lax.dot_general(
                xs[...], g_all[h, rows, :], (((1,), (1,)), ((), ())), preferred_element_type=F32
            )
            for h in range(2)
        ]
        for b in range(3):
            one, two = slice(b * 64, b * 64 + 32), slice(b * 64 + 32, b * 64 + 64)
            three = [taps[1][one], taps[0][one] + taps[1][two], taps[0][two]]
            for a in range(3):
                part[group, :, a * 3 + b] = three[a].reshape(n_width, 2, 128)
        for d in Z_ORDER:
            start(rs_copy(dy, d))

    def sum_along_z(dy):
        group = group_of(dy)
        for d in Z_ORDER:
            rs_copy(dy, d).wait_recv()
        for side in range(2):
            total = part[group, 2 * z + side]
            for d in range(1, n_z):
                total = total + rs_buf[d, group, side]
            part[group, 2 * z + side] = total
        start(pair_copy(dy))

    def hand_out(dy):
        group = group_of(dy)
        pair_copy(dy).wait_recv()
        if dy in BOTH:
            for side in range(2):
                total = part[group, 2 * z + side] + pair_in[dy, side]
                blocks[group, 2 * z + side] = total * factor
        else:
            blocks[group, w] = (part[group, w] + pair_in[dy, 0]) * factor
        for d in Z_ORDER:
            start(ag_copy(dy, w, d, lax.rem(w + 2 * d, n_width)))
        if dy not in BOTH:
            start(ag_copy(dy, w, n_z, across))

    def relay(dy):
        for d in Z_ORDER:
            source = lax.rem(w + n_width - 2 * d, n_width)
            ag_copy(dy, source, d, across).wait_recv()
            if dy not in BOTH:
                start(ag_copy(dy, source, n_z + d, across))

    def f_copy(d):
        return pltpu.make_async_remote_copy(
            src_ref=f_msg.at[lax.rem(k + d, 16)],
            dst_ref=f_all.at[:, own_rows(k), :],
            send_sem=f_send.at[d],
            recv_sem=f_recv.at[d],
            device_id={"chan": lax.rem(k + d, 16)},
            device_id_type=MESH,
        )

    gather_class(0, 0)
    filter_class(0)
    lane = lax.broadcasted_iota(jnp.int32, (96, 128), 1)

    for tile in range(4):
        parts = [
            f_ref[:, b, :, tile * 128 : tile * 128 + 128].reshape(96, 128).astype(F32)
            for b in range(3)
        ]
        for j in range(4):
            out = jnp.zeros((96, 128), F32)
            for b in range(3):
                moved = parts[b]
                if (b - j) % 4:
                    moved = pltpu.roll(moved, ((b - j) % 4) * 32, 1)
                out = jnp.where(lane // 32 == b, moved, out)
            f_msg[tile * 4 + j] = out.astype(BF16).reshape(3, 32, 128)

    f_all[:, own_rows(k), :] = f_msg[k]

    gather_stage(0, 2)
    gather_stage(0, 3)
    gather_class(0, 1)
    filter_class(1)
    gather_class(0, 3)
    filter_class(3)
    gather_stage(0, 4)
    gather_class(0, 2)
    filter_class(2)
    gather_stage(1, 0)
    sum_along_z(0)
    gather_stage(1, 1)
    for d in range(1, 16):
        start(f_copy(d))
    sum_along_z(1)
    hand_out(0)
    sum_along_z(3)
    hand_out(1)
    gather_stage(1, 2)

    lane32 = lax.broadcasted_iota(jnp.int32, (32, cols), 1)

    def edge_copy(which, side, device):
        return pltpu.make_async_remote_copy(
            src_ref=e_out.at[which, side],
            dst_ref=e_in.at[which, side],
            send_sem=e_send.at[which, side],
            recv_sem=e_recv.at[which, side],
            device_id={"width": device},
            device_id_type=MESH,
        )

    def edges_out(which, taps):
        for h in range(2):
            e_out[which, 0, h] = taps[h][0][:, cols - 128 : cols]
            e_out[which, 1, h] = taps[h][2][:, 0:128]
        copies = [edge_copy(which, 0, right), edge_copy(which, 1, left)]
        for copy in copies:
            start(copy)
        for h in range(2):
            moved_right = jnp.where(lane32 == 0, 0.0, pltpu.roll(taps[h][0], 1, 1))
            moved_left = jnp.where(lane32 == cols - 1, 0.0, pltpu.roll(taps[h][2], cols - 1, 1))
            y_buf[which, h] = taps[h][1] + moved_right + moved_left
        return copies

    def edges_in(which, copies, out_ref):
        for copy in copies:
            copy.wait_recv()
        lane128 = lax.broadcasted_iota(jnp.int32, (32, 128), 1)
        for h in range(2):
            came = pltpu.roll(e_in[which, 0, h], 1, 1)
            y_buf[which, h, :, 0:128] += jnp.where((lane128 == 0) & (w > 0), came, 0.0)
            came = pltpu.roll(e_in[which, 1, h], 127, 1)
            y_buf[which, h, :, cols - 128 : cols] += jnp.where(
                (lane128 == 127) & (w < n_width - 1), came, 0.0
            )
            out_ref[h] = y_buf[which, h].astype(BF16)

    sums = None
    for h in range(2):
        block = f_ref[1 - h : 3 - h].reshape(192, f_ref.shape[3])
        term = jnp.dot(block, g_all[h], preferred_element_type=F32)
        sums = term if sums is None else sums + term
    taps = [[sums[h * 96 + b * 32 : h * 96 + b * 32 + 32] for b in (2, 1, 0)] for h in range(2)]
    grad_copies = edges_out(1, taps)

    sum_along_z(2)
    hand_out(3)
    gather_stage(1, 3)
    gather_stage(1, 4)
    hand_out(2)
    relay(0)
    relay(1)
    relay(3)

    for which_dy in range(4):
        gather_class(1, which_dy)
    for d in range(1, 16):
        source = lax.rem(k + 16 - d, 16)
        pltpu.make_async_remote_copy(
            src_ref=f_msg.at[0],
            dst_ref=f_all.at[:, own_rows(source), :],
            send_sem=f_send.at[d],
            recv_sem=f_recv.at[d],
            device_id={"chan": source},
            device_id_type=MESH,
        ).wait_recv()
    depth = f_all.shape[1]
    field = x_all[...].reshape(2 * depth, cols)
    taps = []
    for h in range(2):
        block = f_all[1 - h : 3 - h].reshape(2 * depth, 128)
        sums = lax.dot_general(
            block, field, (((0,), (0,)), ((), ())), preferred_element_type=F32
        )
        taps.append([sums[b * 32 : b * 32 + 32] for b in range(3)])
    conv_copies = edges_out(0, taps)
    relay(2)
    edges_in(1, grad_copies, grad_ref)
    edges_in(0, conv_copies, conv_ref)

    for dy in (0, 1, 3, 2):
        for d in range(0 if dy in BOTH else n_z):
            source = lax.rem(across + n_width - 2 * d, n_width)
            ag_copy(dy, source, n_z + d, across).wait_recv()
    for copy in pending:
        copy.wait_send()


def finish(conv_in, grad_in, blocks, conv_ref, grad_ref, filt_ref):
    for group in range(blocks.shape[0]):
        for tap in range(9):
            filt_ref[tap, :, group * 128 : group * 128 + 128] = blocks[group, :, tap].reshape(
                filt_ref.shape[1], 128
            )
    for source, target in ((conv_in, conv_ref), (grad_in, grad_ref)):
        for h in range(2):
            target[:, h, :] = source[h]


def body(activations, filters, cotangent):
    cin_dev, rows, cols = activations.shape
    n_out = filters.shape[3]
    n_width = lax.axis_size("width")
    factor = 1.0 / math.sqrt(rows * cols * n_width)
    x = jnp.transpose(activations, (1, 0, 2))
    g = jnp.transpose(cotangent, (1, 0, 2))
    f = jnp.transpose(filters, (1, 2, 0, 3))
    vmem = pl.BlockSpec(memory_space=pltpu.VMEM)
    dma = pltpu.SemaphoreType.DMA

    def run(*refs):
        kernel(n_width, factor, *refs)

    conv, grad, filt = pl.pallas_call(
        run,
        out_shape=[
            jax.ShapeDtypeStruct((rows, cin_dev, cols), BF16),
            jax.ShapeDtypeStruct((rows, cin_dev, cols), BF16),
            jax.ShapeDtypeStruct((4, n_width, 9, 2, 128), F32),
        ],
        in_specs=[vmem] * 3,
        out_specs=[vmem] * 3,
        scratch_shapes=[
            pltpu.VMEM((rows, n_out, cols), BF16),
            pltpu.VMEM((rows, n_out, cols), BF16),
            pltpu.VMEM((3, n_out, 128), BF16),
            pltpu.VMEM((16, 3, cin_dev, 128), BF16),
            pltpu.VMEM((2, rows, cin_dev, 128), BF16),
            pltpu.VMEM((192, cols), BF16),
            pltpu.VMEM((4, n_width, 9, 2, 128), F32),
            pltpu.VMEM((4, 2, 9, 2, 128), F32),
            pltpu.VMEM((n_width // 2, 4, 2, 9, 2, 128), F32),
            pltpu.VMEM((2, 2, rows, cin_dev, 128), F32),
            pltpu.VMEM((2, 2, rows, cin_dev, 128), F32),
            pltpu.VMEM((2, rows, cin_dev, cols), F32),
            dma((2, N_MSG)),
            dma((2, N_MSG)),
            dma((16,)),
            dma((16,)),
            dma((2,)),
            dma((2,)),
            dma((4,)),
            dma((4,)),
            dma((4, n_width // 2)),
            dma((4, n_width // 2)),
            dma((4, n_width)),
            dma((4, n_width)),
            dma((2, 2)),
            dma((2, 2)),
        ],
        compiler_params=pltpu.CompilerParams(
            collective_id=0, has_side_effects=True, vmem_limit_bytes=20 * 1024 * 1024
        ),
        name="conv_all",
    )(x, g, f)
    conv, grad, filt = pl.pallas_call(
        finish,
        out_shape=[
            jax.ShapeDtypeStruct((cin_dev, rows, cols), BF16),
            jax.ShapeDtypeStruct((cin_dev, rows, cols), BF16),
            jax.ShapeDtypeStruct((9, cin_dev, n_out), F32),
        ],
        in_specs=[vmem] * 3,
        out_specs=[vmem] * 3,
        compiler_params=pltpu.CompilerParams(vmem_limit_bytes=8 * 1024 * 1024),
        name="finish",
    )(conv, grad, filt)
    filt = jnp.transpose(filt.reshape(3, 3, cin_dev, n_out), (2, 0, 1, 3))
    return conv, grad, filt


def solution(mesh):
    in_specs = (P("chan", None, "width"), P("chan", None, None, None), P("chan", None, "width"))
    out_specs = (P("chan", None, "width"), P("chan", None, "width"), P("chan", None, None, None))
    return jax.shard_map(body, mesh=mesh, in_specs=in_specs, out_specs=out_specs, check_vma=False)
```

```python
import math

import jax
import jax.numpy as jnp
from jax import lax
from jax.experimental import pallas as pl
from jax.experimental.pallas import tpu as pltpu
from jax.sharding import PartitionSpec as P

MESH = pl.DeviceIdType.MESH
BF16 = jnp.bfloat16
F32 = jnp.float32

Y_ONE, Y_TWO, Y_THREE, ACROSS, CORE = (1, 0, 0), (2, 0, 0), (3, 0, 0), (0, 1, 0), (0, 0, 1)
ALONG = [Y_TWO, Y_ONE, Y_THREE]


def arrived(piece, way):
    h, dy, dx, dc = piece
    return (h, (dy - way[0]) % 4, (dx + way[1]) % 2, (dc + way[2]) % 2)


OWN = (0, 0, 0)
STAGES = [
    [
        ((1,) + OWN, [ACROSS]),
        ((0,) + OWN, [ACROSS] + ALONG),
        ((1,) + OWN, ALONG),
        ((0,) + OWN, [CORE]),
        ((1,) + OWN, [CORE]),
    ],
    [
        ((1, 0, 1, 0), ALONG + [CORE]),
        ((0, 0, 1, 0), [CORE]),
    ],
    [
        ((0, 1, 0, 0), [ACROSS, CORE]),
        ((0, 3, 0, 0), [ACROSS, CORE]),
        ((0, 2, 0, 0), [ACROSS, CORE]),
        ((1, 1, 0, 0), [CORE]),
        ((1, 3, 0, 0), [CORE]),
        ((1, 2, 0, 0), [CORE]),
    ],
    [
        ((1, 1, 1, 0), [CORE]),
        ((1, 3, 1, 0), [CORE]),
        ((0, 1, 1, 0), [CORE]),
        ((0, 3, 1, 0), [CORE]),
    ],
    [
        ((1, 2, 1, 0), [CORE]),
        ((0, 2, 1, 0), [CORE]),
    ],
]

STAGES_X = [
    [
        ((1,) + OWN, [ACROSS]),
        ((0,) + OWN, [ACROSS]),
        ((1,) + OWN, ALONG),
        ((0,) + OWN, ALONG),
        ((0,) + OWN, [CORE]),
        ((1,) + OWN, [CORE]),
    ],
    [
        ((1, 0, 1, 0), ALONG + [CORE]),
        ((0, 0, 1, 0), ALONG + [CORE]),
    ],
    [
        ((1, 1, 0, 0), [CORE]),
        ((1, 3, 0, 0), [CORE]),
        ((0, 1, 0, 0), [CORE]),
        ((0, 3, 0, 0), [CORE]),
        ((1, 2, 0, 0), [CORE]),
        ((0, 2, 0, 0), [CORE]),
    ],
    [
        ((1, 1, 1, 0), [CORE]),
        ((1, 3, 1, 0), [CORE]),
        ((0, 1, 1, 0), [CORE]),
        ((0, 3, 1, 0), [CORE]),
    ],
    [
        ((1, 2, 1, 0), [CORE]),
        ((0, 2, 1, 0), [CORE]),
    ],
]


def message_ids(stages):
    number, brings = {}, {}
    for steps in stages:
        for piece, ways in steps:
            for way in ways:
                number[(piece, way)] = len(number)
                brings[arrived(piece, way)] = number[(piece, way)]
    return number, brings


PLANS = [STAGES, STAGES_X]
IDS = [message_ids(stages) for stages in PLANS]
N_MSG = 32
Z_ORDER = [4, 3, 5, 2, 6, 1, 7]
BOTH = (2,)


def kernel(
    n_width,
    factor,
    x_ref,
    g_ref,
    f_ref,
    conv_ref,
    grad_ref,
    blocks,
    x_all,
    g_all,
    f_all,
    f_msg,
    halo,
    xs,
    part,
    pair_in,
    rs_buf,
    e_out,
    e_in,
    y_buf,
    gat_send,
    gat_recv,
    f_send,
    f_recv,
    halo_send,
    halo_recv,
    pair_send,
    pair_recv,
    rs_send,
    rs_recv,
    ag_send,
    ag_recv,
    e_send,
    e_recv,
):
    w = lax.axis_index("width")
    k = lax.axis_index("chan")
    py = k // 4
    px = (k // 2) % 2
    pc = k % 2
    cols = x_ref.shape[2]
    n_z = n_width // 2
    z = w // 2
    column = w % 2
    across = w + 1 - 2 * column
    right = lax.rem(w + 1, n_width)
    left = lax.rem(w + n_width - 1, n_width)

    def chan_of(dy, dx, dc):
        y = lax.rem(py + dy, 4)
        x = 1 - px if dx else px
        c = 1 - pc if dc else pc
        return y * 4 + x * 2 + c

    barrier = pltpu.get_barrier_semaphore()
    for d in range(1, 16):
        pl.semaphore_signal(
            barrier, inc=1, device_id={"chan": lax.rem(k + d, 16)}, device_id_type=MESH
        )
    near_width = [lax.rem(w + 2 * d, n_width) for d in range(1, n_z)] + [right, left]
    for device in near_width:
        pl.semaphore_signal(barrier, inc=1, device_id={"width": device}, device_id_type=MESH)

    def own_rows(index):
        return pl.ds(pl.multiple_of(index * 32, 32), 32)

    pl.semaphore_wait(barrier, 15 + len(near_width))

    pending = []

    def start(copy):
        copy.start()
        pending.append(copy)

    arrays = [(g_all, g_ref), (x_all, x_ref)]

    def piece_ref(which, piece):
        h, dy, dx, dc = piece
        return arrays[which][0].at[h, own_rows(chan_of(dy, dx, dc)), :]

    def gather_send(which, piece, way):
        m = IDS[which][0][(piece, way)]
        ref = piece_ref(which, piece)
        src = arrays[which][1].at[piece[0]] if piece[1:] == OWN else ref
        start(
            pltpu.make_async_remote_copy(
                src_ref=src,
                dst_ref=ref,
                send_sem=gat_send.at[which, m],
                recv_sem=gat_recv.at[which, m],
                device_id={"chan": chan_of(*way)},
                device_id_type=MESH,
            )
        )

    def gather_wait(which, piece):
        m = IDS[which][1][piece]
        ref = piece_ref(which, piece)
        pltpu.make_async_remote_copy(
            src_ref=ref,
            dst_ref=ref,
            send_sem=gat_send.at[which, m],
            recv_sem=gat_recv.at[which, m],
            device_id={"chan": chan_of(*CORE)},
            device_id_type=MESH,
        ).wait_recv()

    def gather_stage(which, number):
        for piece, ways in PLANS[which][number]:
            if piece[1:] != OWN:
                gather_wait(which, piece)
            for way in ways:
                gather_send(which, piece, way)

    def gather_class(which, dy):
        for dx in range(2):
            for h in range(2):
                gather_wait(which, (h, dy, dx, 1))

    def halo_copy(side, device):
        src = x_ref.at[:, :, cols - 128 : cols] if side == 0 else x_ref.at[:, :, 0:128]
        return pltpu.make_async_remote_copy(
            src_ref=src,
            dst_ref=halo.at[side],
            send_sem=halo_send.at[side],
            recv_sem=halo_recv.at[side],
            device_id={"width": device},
            device_id_type=MESH,
        )

    halo_copies = [halo_copy(0, right), halo_copy(1, left)]
    gather_stage(0, 0)
    for copy in halo_copies:
        start(copy)

    x_all[:, own_rows(k), :] = x_ref[...]
    g_all[:, own_rows(k), :] = g_ref[...]

    lane64 = lax.broadcasted_iota(jnp.int32, (64, 128), 1)
    mine = x_ref[...].reshape(64, cols)
    xs[64:128, :] = mine
    mine = mine.astype(F32)
    xs[0:64, :] = pltpu.roll(mine, 1, 1).astype(BF16)
    xs[128:192, :] = pltpu.roll(mine, cols - 1, 1).astype(BF16)
    gather_stage(0, 1)
    for copy in halo_copies:
        copy.wait_recv()
    from_left = jnp.where(w > 0, pltpu.roll(halo[0].reshape(64, 128).astype(F32), 1, 1), 0.0)
    xs[0:64, 0:128] = jnp.where(lane64 == 0, from_left, xs[0:64, 0:128].astype(F32)).astype(BF16)
    from_right = jnp.where(
        w < n_width - 1, pltpu.roll(halo[1].reshape(64, 128).astype(F32), 127, 1), 0.0
    )
    xs[128:192, cols - 128 : cols] = jnp.where(
        lane64 == 127, from_right, xs[128:192, cols - 128 : cols].astype(F32)
    ).astype(BF16)

    def group_of(dy):
        return lax.rem(py + dy, 4)

    def rs_copy(dy, d):
        return pltpu.make_async_remote_copy(
            src_ref=part.at[group_of(dy), pl.ds(2 * lax.rem(z + d, n_z), 2)],
            dst_ref=rs_buf.at[d, group_of(dy)],
            send_sem=rs_send.at[dy, d],
            recv_sem=rs_recv.at[dy, d],
            device_id={"width": lax.rem(w + 2 * d, n_width)},
            device_id_type=MESH,
        )

    def pair_copy(dy):
        return pltpu.make_async_remote_copy(
            src_ref=part.at[group_of(dy), pl.ds(2 * z, 2) if dy in BOTH else pl.ds(across, 1)],
            dst_ref=pair_in.at[dy, pl.ds(0, 2 if dy in BOTH else 1)],
            send_sem=pair_send.at[dy],
            recv_sem=pair_recv.at[dy],
            device_id={"width": across},
            device_id_type=MESH,
        )

    def ag_copy(dy, index, slot, device):
        owners = pl.ds(2 * (index // 2), 2) if dy in BOTH else pl.ds(index, 1)
        ref = blocks.at[group_of(dy), owners]
        return pltpu.make_async_remote_copy(
            src_ref=ref,
            dst_ref=ref,
            send_sem=ag_send.at[dy, slot],
            recv_sem=ag_recv.at[dy, slot],
            device_id={"width": device},
            device_id_type=MESH,
        )

    def filter_class(dy):
        group = group_of(dy)
        rows = pl.ds(pl.multiple_of(group * 128, 128), 128)
        taps = [
            lax.dot_general(
                xs[...], g_all[h, rows, :], (((1,), (1,)), ((), ())), preferred_element_type=F32
            )
            for h in range(2)
        ]
        for b in range(3):
            one, two = slice(b * 64, b * 64 + 32), slice(b * 64 + 32, b * 64 + 64)
            three = [taps[1][one], taps[0][one] + taps[1][two], taps[0][two]]
            for a in range(3):
                part[group, :, a * 3 + b] = three[a].reshape(n_width, 2, 128)
        for d in Z_ORDER:
            start(rs_copy(dy, d))

    def sum_along_z(dy):
        group = group_of(dy)
        for d in Z_ORDER:
            rs_copy(dy, d).wait_recv()
        for side in range(2):
            total = part[group, 2 * z + side]
            for d in range(1, n_z):
                total = total + rs_buf[d, group, side]
            part[group, 2 * z + side] = total
        start(pair_copy(dy))

    def hand_out(dy):
        group = group_of(dy)
        pair_copy(dy).wait_recv()
        if dy in BOTH:
            for side in range(2):
                total = part[group, 2 * z + side] + pair_in[dy, side]
                blocks[group, 2 * z + side] = total * factor
        else:
            blocks[group, w] = (part[group, w] + pair_in[dy, 0]) * factor
        for d in Z_ORDER:
            start(ag_copy(dy, w, d, lax.rem(w + 2 * d, n_width)))
        if dy not in BOTH:
            start(ag_copy(dy, w, n_z, across))

    def relay(dy):
        for d in Z_ORDER:
            source = lax.rem(w + n_width - 2 * d, n_width)
            ag_copy(dy, source, d, across).wait_recv()
            if dy not in BOTH:
                start(ag_copy(dy, source, n_z + d, across))

    def f_copy(d):
        return pltpu.make_async_remote_copy(
            src_ref=f_msg.at[lax.rem(k + d, 16)],
            dst_ref=f_all.at[:, own_rows(k), :],
            send_sem=f_send.at[d],
            recv_sem=f_recv.at[d],
            device_id={"chan": lax.rem(k + d, 16)},
            device_id_type=MESH,
        )

    gather_class(0, 0)
    filter_class(0)
    lane = lax.broadcasted_iota(jnp.int32, (96, 128), 1)

    for tile in range(4):
        parts = [
            f_ref[:, b, :, tile * 128 : tile * 128 + 128].reshape(96, 128).astype(F32)
            for b in range(3)
        ]
        for j in range(4):
            out = jnp.zeros((96, 128), F32)
            for b in range(3):
                moved = parts[b]
                if (b - j) % 4:
                    moved = pltpu.roll(moved, ((b - j) % 4) * 32, 1)
                out = jnp.where(lane // 32 == b, moved, out)
            f_msg[tile * 4 + j] = out.astype(BF16).reshape(3, 32, 128)

    f_all[:, own_rows(k), :] = f_msg[k]

    gather_stage(0, 2)
    gather_stage(0, 3)
    gather_class(0, 1)
    filter_class(1)
    gather_class(0, 3)
    filter_class(3)
    gather_stage(0, 4)
    gather_class(0, 2)
    filter_class(2)
    gather_stage(1, 0)
    sum_along_z(0)
    gather_stage(1, 1)
    for d in range(1, 16):
        start(f_copy(d))
    sum_along_z(1)
    hand_out(0)
    sum_along_z(3)
    gather_stage(1, 2)

    lane32 = lax.broadcasted_iota(jnp.int32, (32, cols), 1)

    def edge_copy(which, side, device):
        return pltpu.make_async_remote_copy(
            src_ref=e_out.at[which, side],
            dst_ref=e_in.at[which, side],
            send_sem=e_send.at[which, side],
            recv_sem=e_recv.at[which, side],
            device_id={"width": device},
            device_id_type=MESH,
        )

    def edges_out(which, taps):
        for h in range(2):
            e_out[which, 0, h] = taps[h][0][:, cols - 128 : cols]
            e_out[which, 1, h] = taps[h][2][:, 0:128]
        copies = [edge_copy(which, 0, right), edge_copy(which, 1, left)]
        for copy in copies:
            start(copy)
        for h in range(2):
            moved_right = jnp.where(lane32 == 0, 0.0, pltpu.roll(taps[h][0], 1, 1))
            moved_left = jnp.where(lane32 == cols - 1, 0.0, pltpu.roll(taps[h][2], cols - 1, 1))
            y_buf[which, h] = taps[h][1] + moved_right + moved_left
        return copies

    def edges_in(which, copies, out_ref):
        for copy in copies:
            copy.wait_recv()
        lane128 = lax.broadcasted_iota(jnp.int32, (32, 128), 1)
        for h in range(2):
            came = pltpu.roll(e_in[which, 0, h], 1, 1)
            y_buf[which, h, :, 0:128] += jnp.where((lane128 == 0) & (w > 0), came, 0.0)
            came = pltpu.roll(e_in[which, 1, h], 127, 1)
            y_buf[which, h, :, cols - 128 : cols] += jnp.where(
                (lane128 == 127) & (w < n_width - 1), came, 0.0
            )
            out_ref[h] = y_buf[which, h].astype(BF16)

    sums = None
    for h in range(2):
        block = f_ref[1 - h : 3 - h].reshape(192, f_ref.shape[3])
        term = jnp.dot(block, g_all[h], preferred_element_type=F32)
        sums = term if sums is None else sums + term
    taps = [[sums[h * 96 + b * 32 : h * 96 + b * 32 + 32] for b in (2, 1, 0)] for h in range(2)]
    grad_copies = edges_out(1, taps)

    sum_along_z(2)
    hand_out(1)
    hand_out(3)
    gather_stage(1, 3)
    gather_stage(1, 4)
    hand_out(2)
    relay(0)
    relay(1)
    relay(3)

    for which_dy in range(4):
        gather_class(1, which_dy)
    for d in range(1, 16):
        source = lax.rem(k + 16 - d, 16)
        pltpu.make_async_remote_copy(
            src_ref=f_msg.at[0],
            dst_ref=f_all.at[:, own_rows(source), :],
            send_sem=f_send.at[d],
            recv_sem=f_recv.at[d],
            device_id={"chan": source},
            device_id_type=MESH,
        ).wait_recv()
    depth = f_all.shape[1]
    field = x_all[...].reshape(2 * depth, cols)
    taps = []
    for h in range(2):
        block = f_all[1 - h : 3 - h].reshape(2 * depth, 128)
        sums = lax.dot_general(
            block, field, (((0,), (0,)), ((), ())), preferred_element_type=F32
        )
        taps.append([sums[b * 32 : b * 32 + 32] for b in range(3)])
    conv_copies = edges_out(0, taps)
    relay(2)
    edges_in(1, grad_copies, grad_ref)
    edges_in(0, conv_copies, conv_ref)

    for dy in (0, 1, 3, 2):
        for d in range(0 if dy in BOTH else n_z):
            source = lax.rem(across + n_width - 2 * d, n_width)
            ag_copy(dy, source, n_z + d, across).wait_recv()
    for copy in pending:
        copy.wait_send()


def finish(conv_in, grad_in, blocks, conv_ref, grad_ref, filt_ref):
    for group in range(blocks.shape[0]):
        for tap in range(9):
            filt_ref[tap, :, group * 128 : group * 128 + 128] = blocks[group, :, tap].reshape(
                filt_ref.shape[1], 128
            )
    for source, target in ((conv_in, conv_ref), (grad_in, grad_ref)):
        for h in range(2):
            target[:, h, :] = source[h]


def body(activations, filters, cotangent):
    cin_dev, rows, cols = activations.shape
    n_out = filters.shape[3]
    n_width = lax.axis_size("width")
    factor = 1.0 / math.sqrt(rows * cols * n_width)
    x = jnp.transpose(activations, (1, 0, 2))
    g = jnp.transpose(cotangent, (1, 0, 2))
    f = jnp.transpose(filters, (1, 2, 0, 3))
    vmem = pl.BlockSpec(memory_space=pltpu.VMEM)
    dma = pltpu.SemaphoreType.DMA

    def run(*refs):
        kernel(n_width, factor, *refs)

    conv, grad, filt = pl.pallas_call(
        run,
        out_shape=[
            jax.ShapeDtypeStruct((rows, cin_dev, cols), BF16),
            jax.ShapeDtypeStruct((rows, cin_dev, cols), BF16),
            jax.ShapeDtypeStruct((4, n_width, 9, 2, 128), F32),
        ],
        in_specs=[vmem] * 3,
        out_specs=[vmem] * 3,
        scratch_shapes=[
            pltpu.VMEM((rows, n_out, cols), BF16),
            pltpu.VMEM((rows, n_out, cols), BF16),
            pltpu.VMEM((3, n_out, 128), BF16),
            pltpu.VMEM((16, 3, cin_dev, 128), BF16),
            pltpu.VMEM((2, rows, cin_dev, 128), BF16),
            pltpu.VMEM((192, cols), BF16),
            pltpu.VMEM((4, n_width, 9, 2, 128), F32),
            pltpu.VMEM((4, 2, 9, 2, 128), F32),
            pltpu.VMEM((n_width // 2, 4, 2, 9, 2, 128), F32),
            pltpu.VMEM((2, 2, rows, cin_dev, 128), F32),
            pltpu.VMEM((2, 2, rows, cin_dev, 128), F32),
            pltpu.VMEM((2, rows, cin_dev, cols), F32),
            dma((2, N_MSG)),
            dma((2, N_MSG)),
            dma((16,)),
            dma((16,)),
            dma((2,)),
            dma((2,)),
            dma((4,)),
            dma((4,)),
            dma((4, n_width // 2)),
            dma((4, n_width // 2)),
            dma((4, n_width)),
            dma((4, n_width)),
            dma((2, 2)),
            dma((2, 2)),
        ],
        compiler_params=pltpu.CompilerParams(
            collective_id=0, has_side_effects=True, vmem_limit_bytes=20 * 1024 * 1024
        ),
        name="conv_all",
    )(x, g, f)
    conv, grad, filt = pl.pallas_call(
        finish,
        out_shape=[
            jax.ShapeDtypeStruct((cin_dev, rows, cols), BF16),
            jax.ShapeDtypeStruct((cin_dev, rows, cols), BF16),
            jax.ShapeDtypeStruct((9, cin_dev, n_out), F32),
        ],
        in_specs=[vmem] * 3,
        out_specs=[vmem] * 3,
        compiler_params=pltpu.CompilerParams(vmem_limit_bytes=8 * 1024 * 1024),
        name="finish",
    )(conv, grad, filt)
    filt = jnp.transpose(filt.reshape(3, 3, cin_dev, n_out), (2, 0, 1, 3))
    return conv, grad, filt


def solution(mesh):
    in_specs = (P("chan", None, "width"), P("chan", None, None, None), P("chan", None, "width"))
    out_specs = (P("chan", None, "width"), P("chan", None, "width"), P("chan", None, None, None))
    return jax.shard_map(body, mesh=mesh, in_specs=in_specs, out_specs=out_specs, check_vma=False)
```

```python
import math

import jax
import jax.numpy as jnp
from jax import lax
from jax.experimental import pallas as pl
from jax.experimental.pallas import tpu as pltpu
from jax.sharding import PartitionSpec as P

MESH = pl.DeviceIdType.MESH
BF16 = jnp.bfloat16
F32 = jnp.float32

Y_ONE, Y_TWO, Y_THREE, ACROSS, CORE = (1, 0, 0), (2, 0, 0), (3, 0, 0), (0, 1, 0), (0, 0, 1)
ALONG = [Y_TWO, Y_ONE, Y_THREE]


def arrived(piece, way):
    h, dy, dx, dc = piece
    return (h, (dy - way[0]) % 4, (dx + way[1]) % 2, (dc + way[2]) % 2)


OWN = (0, 0, 0)
STAGES = [
    [
        ((1,) + OWN, [ACROSS]),
        ((0,) + OWN, [ACROSS] + ALONG),
        ((1,) + OWN, ALONG),
        ((0,) + OWN, [CORE]),
        ((1,) + OWN, [CORE]),
    ],
    [
        ((1, 0, 1, 0), ALONG + [CORE]),
        ((0, 0, 1, 0), [CORE]),
    ],
    [
        ((0, 1, 0, 0), [ACROSS, CORE]),
        ((0, 3, 0, 0), [ACROSS, CORE]),
        ((0, 2, 0, 0), [ACROSS, CORE]),
        ((1, 1, 0, 0), [CORE]),
        ((1, 3, 0, 0), [CORE]),
        ((1, 2, 0, 0), [CORE]),
    ],
    [
        ((1, 1, 1, 0), [CORE]),
        ((1, 3, 1, 0), [CORE]),
        ((0, 1, 1, 0), [CORE]),
        ((0, 3, 1, 0), [CORE]),
    ],
    [
        ((1, 2, 1, 0), [CORE]),
        ((0, 2, 1, 0), [CORE]),
    ],
]

STAGES_X = [
    [
        ((1,) + OWN, [ACROSS]),
        ((0,) + OWN, [ACROSS]),
        ((1,) + OWN, ALONG),
        ((0,) + OWN, ALONG),
        ((0,) + OWN, [CORE]),
        ((1,) + OWN, [CORE]),
    ],
    [
        ((1, 0, 1, 0), ALONG + [CORE]),
        ((0, 0, 1, 0), ALONG + [CORE]),
    ],
    [
        ((1, 1, 0, 0), [CORE]),
        ((1, 3, 0, 0), [CORE]),
        ((0, 1, 0, 0), [CORE]),
        ((0, 3, 0, 0), [CORE]),
        ((1, 2, 0, 0), [CORE]),
        ((0, 2, 0, 0), [CORE]),
    ],
    [
        ((1, 1, 1, 0), [CORE]),
        ((1, 3, 1, 0), [CORE]),
        ((0, 1, 1, 0), [CORE]),
        ((0, 3, 1, 0), [CORE]),
    ],
    [
        ((1, 2, 1, 0), [CORE]),
        ((0, 2, 1, 0), [CORE]),
    ],
]


def message_ids(stages):
    number, brings = {}, {}
    for steps in stages:
        for piece, ways in steps:
            for way in ways:
                number[(piece, way)] = len(number)
                brings[arrived(piece, way)] = number[(piece, way)]
    return number, brings


PLANS = [STAGES, STAGES_X]
IDS = [message_ids(stages) for stages in PLANS]
N_MSG = 32
Z_ORDER = [4, 3, 5, 2, 6, 1, 7]
FAR_FIRST = [(y, x, c) for y in (2, 1, 3, 0) for x in (1, 0) for c in (1, 0) if (y, x, c) != (0, 0, 0)]
BOTH = (2,)


def kernel(
    n_width,
    factor,
    x_ref,
    g_ref,
    f_ref,
    conv_ref,
    grad_ref,
    blocks,
    x_all,
    g_all,
    f_all,
    f_msg,
    halo,
    xs,
    part,
    pair_in,
    rs_buf,
    e_out,
    e_in,
    y_buf,
    gat_send,
    gat_recv,
    f_send,
    f_recv,
    halo_send,
    halo_recv,
    pair_send,
    pair_recv,
    rs_send,
    rs_recv,
    ag_send,
    ag_recv,
    e_send,
    e_recv,
):
    w = lax.axis_index("width")
    k = lax.axis_index("chan")
    py = k // 4
    px = (k // 2) % 2
    pc = k % 2
    cols = x_ref.shape[2]
    n_z = n_width // 2
    z = w // 2
    column = w % 2
    across = w + 1 - 2 * column
    right = lax.rem(w + 1, n_width)
    left = lax.rem(w + n_width - 1, n_width)

    def chan_of(dy, dx, dc):
        y = lax.rem(py + dy, 4)
        x = 1 - px if dx else px
        c = 1 - pc if dc else pc
        return y * 4 + x * 2 + c

    barrier = pltpu.get_barrier_semaphore()
    near_width = [lax.rem(w + 2 * d, n_width) for d in Z_ORDER] + [right, left]
    for device in near_width:
        pl.semaphore_signal(barrier, inc=1, device_id={"width": device}, device_id_type=MESH)
    for way in FAR_FIRST:
        pl.semaphore_signal(barrier, inc=1, device_id={"chan": chan_of(*way)}, device_id_type=MESH)

    def own_rows(index):
        return pl.ds(pl.multiple_of(index * 32, 32), 32)

    pl.semaphore_wait(barrier, 15 + len(near_width))

    pending = []

    def start(copy):
        copy.start()
        pending.append(copy)

    arrays = [(g_all, g_ref), (x_all, x_ref)]

    def piece_ref(which, piece):
        h, dy, dx, dc = piece
        return arrays[which][0].at[h, own_rows(chan_of(dy, dx, dc)), :]

    def gather_send(which, piece, way):
        m = IDS[which][0][(piece, way)]
        ref = piece_ref(which, piece)
        src = arrays[which][1].at[piece[0]] if piece[1:] == OWN else ref
        start(
            pltpu.make_async_remote_copy(
                src_ref=src,
                dst_ref=ref,
                send_sem=gat_send.at[which, m],
                recv_sem=gat_recv.at[which, m],
                device_id={"chan": chan_of(*way)},
                device_id_type=MESH,
            )
        )

    def gather_wait(which, piece):
        m = IDS[which][1][piece]
        ref = piece_ref(which, piece)
        pltpu.make_async_remote_copy(
            src_ref=ref,
            dst_ref=ref,
            send_sem=gat_send.at[which, m],
            recv_sem=gat_recv.at[which, m],
            device_id={"chan": chan_of(*CORE)},
            device_id_type=MESH,
        ).wait_recv()

    def gather_stage(which, number):
        for piece, ways in PLANS[which][number]:
            if piece[1:] != OWN:
                gather_wait(which, piece)
            for way in ways:
                gather_send(which, piece, way)

    def gather_class(which, dy):
        for dx in range(2):
            for h in range(2):
                gather_wait(which, (h, dy, dx, 1))

    def halo_copy(side, device):
        src = x_ref.at[:, :, cols - 128 : cols] if side == 0 else x_ref.at[:, :, 0:128]
        return pltpu.make_async_remote_copy(
            src_ref=src,
            dst_ref=halo.at[side],
            send_sem=halo_send.at[side],
            recv_sem=halo_recv.at[side],
            device_id={"width": device},
            device_id_type=MESH,
        )

    halo_copies = [halo_copy(0, right), halo_copy(1, left)]
    gather_stage(0, 0)
    for copy in halo_copies:
        start(copy)

    x_all[:, own_rows(k), :] = x_ref[...]
    g_all[:, own_rows(k), :] = g_ref[...]

    lane64 = lax.broadcasted_iota(jnp.int32, (64, 128), 1)
    mine = x_ref[...].reshape(64, cols)
    xs[64:128, :] = mine
    mine = mine.astype(F32)
    xs[0:64, :] = pltpu.roll(mine, 1, 1).astype(BF16)
    xs[128:192, :] = pltpu.roll(mine, cols - 1, 1).astype(BF16)
    gather_stage(0, 1)
    for copy in halo_copies:
        copy.wait_recv()
    from_left = jnp.where(w > 0, pltpu.roll(halo[0].reshape(64, 128).astype(F32), 1, 1), 0.0)
    xs[0:64, 0:128] = jnp.where(lane64 == 0, from_left, xs[0:64, 0:128].astype(F32)).astype(BF16)
    from_right = jnp.where(
        w < n_width - 1, pltpu.roll(halo[1].reshape(64, 128).astype(F32), 127, 1), 0.0
    )
    xs[128:192, cols - 128 : cols] = jnp.where(
        lane64 == 127, from_right, xs[128:192, cols - 128 : cols].astype(F32)
    ).astype(BF16)

    def group_of(dy):
        return lax.rem(py + dy, 4)

    def rs_copy(dy, d):
        return pltpu.make_async_remote_copy(
            src_ref=part.at[group_of(dy), pl.ds(2 * lax.rem(z + d, n_z), 2)],
            dst_ref=rs_buf.at[d, group_of(dy)],
            send_sem=rs_send.at[dy, d],
            recv_sem=rs_recv.at[dy, d],
            device_id={"width": lax.rem(w + 2 * d, n_width)},
            device_id_type=MESH,
        )

    def pair_copy(dy):
        return pltpu.make_async_remote_copy(
            src_ref=part.at[group_of(dy), pl.ds(2 * z, 2) if dy in BOTH else pl.ds(across, 1)],
            dst_ref=pair_in.at[dy, pl.ds(0, 2 if dy in BOTH else 1)],
            send_sem=pair_send.at[dy],
            recv_sem=pair_recv.at[dy],
            device_id={"width": across},
            device_id_type=MESH,
        )

    def ag_copy(dy, index, slot, device):
        owners = pl.ds(2 * (index // 2), 2) if dy in BOTH else pl.ds(index, 1)
        ref = blocks.at[group_of(dy), owners]
        return pltpu.make_async_remote_copy(
            src_ref=ref,
            dst_ref=ref,
            send_sem=ag_send.at[dy, slot],
            recv_sem=ag_recv.at[dy, slot],
            device_id={"width": device},
            device_id_type=MESH,
        )

    def filter_class(dy):
        group = group_of(dy)
        rows = pl.ds(pl.multiple_of(group * 128, 128), 128)
        taps = [
            lax.dot_general(
                xs[...], g_all[h, rows, :], (((1,), (1,)), ((), ())), preferred_element_type=F32
            )
            for h in range(2)
        ]
        for b in range(3):
            one, two = slice(b * 64, b * 64 + 32), slice(b * 64 + 32, b * 64 + 64)
            three = [taps[1][one], taps[0][one] + taps[1][two], taps[0][two]]
            for a in range(3):
                part[group, :, a * 3 + b] = three[a].reshape(n_width, 2, 128)
        for d in Z_ORDER:
            start(rs_copy(dy, d))

    def sum_along_z(dy):
        group = group_of(dy)
        for d in Z_ORDER:
            rs_copy(dy, d).wait_recv()
        for side in range(2):
            total = part[group, 2 * z + side]
            for d in range(1, n_z):
                total = total + rs_buf[d, group, side]
            part[group, 2 * z + side] = total
        start(pair_copy(dy))

    def hand_out(dy):
        group = group_of(dy)
        pair_copy(dy).wait_recv()
        if dy in BOTH:
            for side in range(2):
                total = part[group, 2 * z + side] + pair_in[dy, side]
                blocks[group, 2 * z + side] = total * factor
        else:
            blocks[group, w] = (part[group, w] + pair_in[dy, 0]) * factor
        for d in Z_ORDER:
            start(ag_copy(dy, w, d, lax.rem(w + 2 * d, n_width)))
        if dy not in BOTH:
            start(ag_copy(dy, w, n_z, across))

    def relay(dy):
        for d in Z_ORDER:
            source = lax.rem(w + n_width - 2 * d, n_width)
            ag_copy(dy, source, d, across).wait_recv()
            if dy not in BOTH:
                start(ag_copy(dy, source, n_z + d, across))

    def f_copy(d):
        return pltpu.make_async_remote_copy(
            src_ref=f_msg.at[lax.rem(k + d, 16)],
            dst_ref=f_all.at[:, own_rows(k), :],
            send_sem=f_send.at[d],
            recv_sem=f_recv.at[d],
            device_id={"chan": lax.rem(k + d, 16)},
            device_id_type=MESH,
        )

    gather_class(0, 0)
    filter_class(0)
    lane = lax.broadcasted_iota(jnp.int32, (96, 128), 1)

    for tile in range(4):
        parts = [
            f_ref[:, b, :, tile * 128 : tile * 128 + 128].reshape(96, 128).astype(F32)
            for b in range(3)
        ]
        for j in range(4):
            out = jnp.zeros((96, 128), F32)
            for b in range(3):
                moved = parts[b]
                if (b - j) % 4:
                    moved = pltpu.roll(moved, ((b - j) % 4) * 32, 1)
                out = jnp.where(lane // 32 == b, moved, out)
            f_msg[tile * 4 + j] = out.astype(BF16).reshape(3, 32, 128)

    f_all[:, own_rows(k), :] = f_msg[k]

    gather_stage(0, 2)
    gather_stage(0, 3)
    gather_class(0, 1)
    filter_class(1)
    gather_class(0, 3)
    filter_class(3)
    gather_stage(0, 4)
    gather_class(0, 2)
    filter_class(2)
    gather_stage(1, 0)
    sum_along_z(0)
    gather_stage(1, 1)
    for d in range(1, 16):
        start(f_copy(d))
    sum_along_z(1)
    hand_out(0)
    sum_along_z(3)
    gather_stage(1, 2)

    lane32 = lax.broadcasted_iota(jnp.int32, (32, cols), 1)

    def edge_copy(which, side, device):
        return pltpu.make_async_remote_copy(
            src_ref=e_out.at[which, side],
            dst_ref=e_in.at[which, side],
            send_sem=e_send.at[which, side],
            recv_sem=e_recv.at[which, side],
            device_id={"width": device},
            device_id_type=MESH,
        )

    def edges_out(which, taps):
        for h in range(2):
            e_out[which, 0, h] = taps[h][0][:, cols - 128 : cols]
            e_out[which, 1, h] = taps[h][2][:, 0:128]
        copies = [edge_copy(which, 0, right), edge_copy(which, 1, left)]
        for copy in copies:
            start(copy)
        for h in range(2):
            moved_right = jnp.where(lane32 == 0, 0.0, pltpu.roll(taps[h][0], 1, 1))
            moved_left = jnp.where(lane32 == cols - 1, 0.0, pltpu.roll(taps[h][2], cols - 1, 1))
            y_buf[which, h] = taps[h][1] + moved_right + moved_left
        return copies

    def edges_in(which, copies, out_ref):
        for copy in copies:
            copy.wait_recv()
        lane128 = lax.broadcasted_iota(jnp.int32, (32, 128), 1)
        for h in range(2):
            came = pltpu.roll(e_in[which, 0, h], 1, 1)
            y_buf[which, h, :, 0:128] += jnp.where((lane128 == 0) & (w > 0), came, 0.0)
            came = pltpu.roll(e_in[which, 1, h], 127, 1)
            y_buf[which, h, :, cols - 128 : cols] += jnp.where(
                (lane128 == 127) & (w < n_width - 1), came, 0.0
            )
            out_ref[h] = y_buf[which, h].astype(BF16)

    sums = None
    for h in range(2):
        block = f_ref[1 - h : 3 - h].reshape(192, f_ref.shape[3])
        term = jnp.dot(block, g_all[h], preferred_element_type=F32)
        sums = term if sums is None else sums + term
    taps = [[sums[h * 96 + b * 32 : h * 96 + b * 32 + 32] for b in (2, 1, 0)] for h in range(2)]
    grad_copies = edges_out(1, taps)

    sum_along_z(2)
    hand_out(1)
    hand_out(3)
    gather_stage(1, 3)
    gather_stage(1, 4)
    hand_out(2)
    relay(0)
    relay(1)
    relay(3)

    for which_dy in range(4):
        gather_class(1, which_dy)
    for d in range(1, 16):
        source = lax.rem(k + 16 - d, 16)
        pltpu.make_async_remote_copy(
            src_ref=f_msg.at[0],
            dst_ref=f_all.at[:, own_rows(source), :],
            send_sem=f_send.at[d],
            recv_sem=f_recv.at[d],
            device_id={"chan": source},
            device_id_type=MESH,
        ).wait_recv()
    depth = f_all.shape[1]
    field = x_all[...].reshape(2 * depth, cols)
    taps = []
    for h in range(2):
        block = f_all[1 - h : 3 - h].reshape(2 * depth, 128)
        sums = lax.dot_general(
            block, field, (((0,), (0,)), ((), ())), preferred_element_type=F32
        )
        taps.append([sums[b * 32 : b * 32 + 32] for b in range(3)])
    conv_copies = edges_out(0, taps)
    relay(2)
    edges_in(1, grad_copies, grad_ref)
    edges_in(0, conv_copies, conv_ref)

    for dy in (0, 1, 3, 2):
        for d in range(0 if dy in BOTH else n_z):
            source = lax.rem(across + n_width - 2 * d, n_width)
            ag_copy(dy, source, n_z + d, across).wait_recv()
    for copy in pending:
        copy.wait_send()


def finish(conv_in, grad_in, blocks, conv_ref, grad_ref, filt_ref):
    for group in range(blocks.shape[0]):
        for tap in range(9):
            filt_ref[tap, :, group * 128 : group * 128 + 128] = blocks[group, :, tap].reshape(
                filt_ref.shape[1], 128
            )
    for source, target in ((conv_in, conv_ref), (grad_in, grad_ref)):
        for h in range(2):
            target[:, h, :] = source[h]


def body(activations, filters, cotangent):
    cin_dev, rows, cols = activations.shape
    n_out = filters.shape[3]
    n_width = lax.axis_size("width")
    factor = 1.0 / math.sqrt(rows * cols * n_width)
    x = jnp.transpose(activations, (1, 0, 2))
    g = jnp.transpose(cotangent, (1, 0, 2))
    f = jnp.transpose(filters, (1, 2, 0, 3))
    vmem = pl.BlockSpec(memory_space=pltpu.VMEM)
    dma = pltpu.SemaphoreType.DMA

    def run(*refs):
        kernel(n_width, factor, *refs)

    conv, grad, filt = pl.pallas_call(
        run,
        out_shape=[
            jax.ShapeDtypeStruct((rows, cin_dev, cols), BF16),
            jax.ShapeDtypeStruct((rows, cin_dev, cols), BF16),
            jax.ShapeDtypeStruct((4, n_width, 9, 2, 128), F32),
        ],
        in_specs=[vmem] * 3,
        out_specs=[vmem] * 3,
        scratch_shapes=[
            pltpu.VMEM((rows, n_out, cols), BF16),
            pltpu.VMEM((rows, n_out, cols), BF16),
            pltpu.VMEM((3, n_out, 128), BF16),
            pltpu.VMEM((16, 3, cin_dev, 128), BF16),
            pltpu.VMEM((2, rows, cin_dev, 128), BF16),
            pltpu.VMEM((192, cols), BF16),
            pltpu.VMEM((4, n_width, 9, 2, 128), F32),
            pltpu.VMEM((4, 2, 9, 2, 128), F32),
            pltpu.VMEM((n_width // 2, 4, 2, 9, 2, 128), F32),
            pltpu.VMEM((2, 2, rows, cin_dev, 128), F32),
            pltpu.VMEM((2, 2, rows, cin_dev, 128), F32),
            pltpu.VMEM((2, rows, cin_dev, cols), F32),
            dma((2, N_MSG)),
            dma((2, N_MSG)),
            dma((16,)),
            dma((16,)),
            dma((2,)),
            dma((2,)),
            dma((4,)),
            dma((4,)),
            dma((4, n_width // 2)),
            dma((4, n_width // 2)),
            dma((4, n_width)),
            dma((4, n_width)),
            dma((2, 2)),
            dma((2, 2)),
        ],
        compiler_params=pltpu.CompilerParams(
            collective_id=0, has_side_effects=True, vmem_limit_bytes=20 * 1024 * 1024
        ),
        name="conv_all",
    )(x, g, f)
    conv, grad, filt = pl.pallas_call(
        finish,
        out_shape=[
            jax.ShapeDtypeStruct((cin_dev, rows, cols), BF16),
            jax.ShapeDtypeStruct((cin_dev, rows, cols), BF16),
            jax.ShapeDtypeStruct((9, cin_dev, n_out), F32),
        ],
        in_specs=[vmem] * 3,
        out_specs=[vmem] * 3,
        compiler_params=pltpu.CompilerParams(vmem_limit_bytes=8 * 1024 * 1024),
        name="finish",
    )(conv, grad, filt)
    filt = jnp.transpose(filt.reshape(3, 3, cin_dev, n_out), (2, 0, 1, 3))
    return conv, grad, filt


def solution(mesh):
    in_specs = (P("chan", None, "width"), P("chan", None, None, None), P("chan", None, "width"))
    out_specs = (P("chan", None, "width"), P("chan", None, "width"), P("chan", None, None, None))
    return jax.shard_map(body, mesh=mesh, in_specs=in_specs, out_specs=out_specs, check_vma=False)
```

```python
import math

import jax
import jax.numpy as jnp
from jax import lax
from jax.experimental import pallas as pl
from jax.experimental.pallas import tpu as pltpu
from jax.sharding import PartitionSpec as P

MESH = pl.DeviceIdType.MESH
BF16 = jnp.bfloat16
F32 = jnp.float32

Y_ONE, Y_TWO, Y_THREE, ACROSS, CORE = (1, 0, 0), (2, 0, 0), (3, 0, 0), (0, 1, 0), (0, 0, 1)
ALONG = [Y_TWO, Y_ONE, Y_THREE]


def arrived(piece, way):
    h, dy, dx, dc = piece
    return (h, (dy - way[0]) % 4, (dx + way[1]) % 2, (dc + way[2]) % 2)


OWN = (0, 0, 0)
STAGES = [
    [
        ((1,) + OWN, [ACROSS]),
        ((0,) + OWN, [ACROSS] + ALONG),
        ((1,) + OWN, ALONG),
        ((0,) + OWN, [CORE]),
        ((1,) + OWN, [CORE]),
    ],
    [
        ((1, 0, 1, 0), ALONG + [CORE]),
        ((0, 0, 1, 0), [CORE]),
    ],
    [
        ((0, 1, 0, 0), [ACROSS, CORE]),
        ((0, 3, 0, 0), [ACROSS, CORE]),
        ((0, 2, 0, 0), [ACROSS, CORE]),
        ((1, 1, 0, 0), [CORE]),
        ((1, 3, 0, 0), [CORE]),
        ((1, 2, 0, 0), [CORE]),
    ],
    [
        ((1, 1, 1, 0), [CORE]),
        ((1, 3, 1, 0), [CORE]),
        ((0, 1, 1, 0), [CORE]),
        ((0, 3, 1, 0), [CORE]),
    ],
    [
        ((1, 2, 1, 0), [CORE]),
        ((0, 2, 1, 0), [CORE]),
    ],
]

STAGES_X = [
    [
        ((1,) + OWN, [ACROSS]),
        ((0,) + OWN, [ACROSS]),
        ((1,) + OWN, ALONG),
        ((0,) + OWN, ALONG),
        ((0,) + OWN, [CORE]),
        ((1,) + OWN, [CORE]),
    ],
    [
        ((1, 0, 1, 0), ALONG + [CORE]),
        ((0, 0, 1, 0), ALONG + [CORE]),
    ],
    [
        ((1, 1, 0, 0), [CORE]),
        ((1, 3, 0, 0), [CORE]),
        ((0, 1, 0, 0), [CORE]),
        ((0, 3, 0, 0), [CORE]),
        ((1, 2, 0, 0), [CORE]),
        ((0, 2, 0, 0), [CORE]),
    ],
    [
        ((1, 1, 1, 0), [CORE]),
        ((1, 3, 1, 0), [CORE]),
        ((0, 1, 1, 0), [CORE]),
        ((0, 3, 1, 0), [CORE]),
    ],
    [
        ((1, 2, 1, 0), [CORE]),
        ((0, 2, 1, 0), [CORE]),
    ],
]


def message_ids(stages):
    number, brings = {}, {}
    for steps in stages:
        for piece, ways in steps:
            for way in ways:
                number[(piece, way)] = len(number)
                brings[arrived(piece, way)] = number[(piece, way)]
    return number, brings


PLANS = [STAGES, STAGES_X]
IDS = [message_ids(stages) for stages in PLANS]
N_MSG = 32
Z_ORDER = [4, 3, 5, 2, 6, 1, 7]
FAR_FIRST = [(y, x, c) for y in (2, 1, 3, 0) for x in (1, 0) for c in (1, 0) if (y, x, c) != (0, 0, 0)]
BOTH = (2,)


def kernel(
    n_width,
    factor,
    x_ref,
    g_ref,
    f_ref,
    conv_ref,
    grad_ref,
    blocks,
    x_all,
    g_all,
    f_all,
    f_msg,
    halo,
    xs,
    part,
    pair_in,
    rs_buf,
    e_out,
    e_in,
    y_buf,
    gat_send,
    gat_recv,
    f_send,
    f_recv,
    halo_send,
    halo_recv,
    pair_send,
    pair_recv,
    rs_send,
    rs_recv,
    ag_send,
    ag_recv,
    e_send,
    e_recv,
):
    w = lax.axis_index("width")
    k = lax.axis_index("chan")
    py = k // 4
    px = (k // 2) % 2
    pc = k % 2
    cols = x_ref.shape[2]
    n_z = n_width // 2
    z = w // 2
    column = w % 2
    across = w + 1 - 2 * column
    right = lax.rem(w + 1, n_width)
    left = lax.rem(w + n_width - 1, n_width)

    def chan_of(dy, dx, dc):
        y = lax.rem(py + dy, 4)
        x = 1 - px if dx else px
        c = 1 - pc if dc else pc
        return y * 4 + x * 2 + c

    barrier = pltpu.get_barrier_semaphore()
    near_width = [lax.rem(w + 2 * d, n_width) for d in Z_ORDER] + [right, left]
    for device in near_width:
        pl.semaphore_signal(barrier, inc=1, device_id={"width": device}, device_id_type=MESH)
    for way in FAR_FIRST:
        pl.semaphore_signal(barrier, inc=1, device_id={"chan": chan_of(*way)}, device_id_type=MESH)

    def own_rows(index):
        return pl.ds(pl.multiple_of(index * 32, 32), 32)

    pl.semaphore_wait(barrier, 15 + len(near_width))

    pending = []

    def start(copy):
        copy.start()
        pending.append(copy)

    arrays = [(g_all, g_ref), (x_all, x_ref)]

    def piece_ref(which, piece):
        h, dy, dx, dc = piece
        return arrays[which][0].at[h, own_rows(chan_of(dy, dx, dc)), :]

    def gather_send(which, piece, way):
        m = IDS[which][0][(piece, way)]
        ref = piece_ref(which, piece)
        src = arrays[which][1].at[piece[0]] if piece[1:] == OWN else ref
        start(
            pltpu.make_async_remote_copy(
                src_ref=src,
                dst_ref=ref,
                send_sem=gat_send.at[which, m],
                recv_sem=gat_recv.at[which, m],
                device_id={"chan": chan_of(*way)},
                device_id_type=MESH,
            )
        )

    def gather_wait(which, piece):
        m = IDS[which][1][piece]
        ref = piece_ref(which, piece)
        pltpu.make_async_remote_copy(
            src_ref=ref,
            dst_ref=ref,
            send_sem=gat_send.at[which, m],
            recv_sem=gat_recv.at[which, m],
            device_id={"chan": chan_of(*CORE)},
            device_id_type=MESH,
        ).wait_recv()

    def gather_stage(which, number):
        for piece, ways in PLANS[which][number]:
            if piece[1:] != OWN:
                gather_wait(which, piece)
            for way in ways:
                gather_send(which, piece, way)

    def gather_class(which, dy):
        for dx in range(2):
            for h in range(2):
                gather_wait(which, (h, dy, dx, 1))

    def halo_copy(side, device):
        src = x_ref.at[:, :, cols - 128 : cols] if side == 0 else x_ref.at[:, :, 0:128]
        return pltpu.make_async_remote_copy(
            src_ref=src,
            dst_ref=halo.at[side],
            send_sem=halo_send.at[side],
            recv_sem=halo_recv.at[side],
            device_id={"width": device},
            device_id_type=MESH,
        )

    halo_copies = [halo_copy(0, right), halo_copy(1, left)]
    gather_stage(0, 0)
    for copy in halo_copies:
        start(copy)

    x_all[:, own_rows(k), :] = x_ref[...]
    g_all[:, own_rows(k), :] = g_ref[...]

    lane64 = lax.broadcasted_iota(jnp.int32, (64, 128), 1)
    mine = x_ref[...].reshape(64, cols)
    xs[64:128, :] = mine
    mine = mine.astype(F32)
    xs[0:64, :] = pltpu.roll(mine, 1, 1).astype(BF16)
    xs[128:192, :] = pltpu.roll(mine, cols - 1, 1).astype(BF16)
    gather_stage(0, 1)
    for copy in halo_copies:
        copy.wait_recv()
    from_left = jnp.where(w > 0, pltpu.roll(halo[0].reshape(64, 128).astype(F32), 1, 1), 0.0)
    xs[0:64, 0:128] = jnp.where(lane64 == 0, from_left, xs[0:64, 0:128].astype(F32)).astype(BF16)
    from_right = jnp.where(
        w < n_width - 1, pltpu.roll(halo[1].reshape(64, 128).astype(F32), 127, 1), 0.0
    )
    xs[128:192, cols - 128 : cols] = jnp.where(
        lane64 == 127, from_right, xs[128:192, cols - 128 : cols].astype(F32)
    ).astype(BF16)

    def group_of(dy):
        return lax.rem(py + dy, 4)

    def rs_copy(dy, d):
        return pltpu.make_async_remote_copy(
            src_ref=part.at[group_of(dy), pl.ds(2 * lax.rem(z + d, n_z), 2)],
            dst_ref=rs_buf.at[d, group_of(dy)],
            send_sem=rs_send.at[dy, d],
            recv_sem=rs_recv.at[dy, d],
            device_id={"width": lax.rem(w + 2 * d, n_width)},
            device_id_type=MESH,
        )

    def pair_copy(dy):
        return pltpu.make_async_remote_copy(
            src_ref=part.at[group_of(dy), pl.ds(2 * z, 2) if dy in BOTH else pl.ds(across, 1)],
            dst_ref=pair_in.at[dy, pl.ds(0, 2 if dy in BOTH else 1)],
            send_sem=pair_send.at[dy],
            recv_sem=pair_recv.at[dy],
            device_id={"width": across},
            device_id_type=MESH,
        )

    def ag_copy(dy, index, slot, device):
        owners = pl.ds(2 * (index // 2), 2) if dy in BOTH else pl.ds(index, 1)
        ref = blocks.at[group_of(dy), owners]
        return pltpu.make_async_remote_copy(
            src_ref=ref,
            dst_ref=ref,
            send_sem=ag_send.at[dy, slot],
            recv_sem=ag_recv.at[dy, slot],
            device_id={"width": device},
            device_id_type=MESH,
        )

    def filter_class(dy):
        group = group_of(dy)
        rows = pl.ds(pl.multiple_of(group * 128, 128), 128)
        taps = [
            lax.dot_general(
                xs[...], g_all[h, rows, :], (((1,), (1,)), ((), ())), preferred_element_type=F32
            )
            for h in range(2)
        ]
        for b in range(3):
            one, two = slice(b * 64, b * 64 + 32), slice(b * 64 + 32, b * 64 + 64)
            three = [taps[1][one], taps[0][one] + taps[1][two], taps[0][two]]
            for a in range(3):
                part[group, :, a * 3 + b] = three[a].reshape(n_width, 2, 128)
        for d in Z_ORDER:
            start(rs_copy(dy, d))

    def sum_along_z(dy):
        group = group_of(dy)
        for d in Z_ORDER:
            rs_copy(dy, d).wait_recv()
        for side in range(2):
            total = part[group, 2 * z + side]
            for d in range(1, n_z):
                total = total + rs_buf[d, group, side]
            part[group, 2 * z + side] = total
        start(pair_copy(dy))

    def hand_out(dy):
        group = group_of(dy)
        pair_copy(dy).wait_recv()
        if dy in BOTH:
            for side in range(2):
                total = part[group, 2 * z + side] + pair_in[dy, side]
                blocks[group, 2 * z + side] = total * factor
        else:
            blocks[group, w] = (part[group, w] + pair_in[dy, 0]) * factor
        for d in Z_ORDER:
            start(ag_copy(dy, w, d, lax.rem(w + 2 * d, n_width)))
        if dy not in BOTH:
            start(ag_copy(dy, w, n_z, across))

    def relay(dy):
        for d in Z_ORDER:
            source = lax.rem(w + n_width - 2 * d, n_width)
            ag_copy(dy, source, d, across).wait_recv()
            if dy not in BOTH:
                start(ag_copy(dy, source, n_z + d, across))

    def f_copy(d):
        return pltpu.make_async_remote_copy(
            src_ref=f_msg.at[lax.rem(k + d, 16)],
            dst_ref=f_all.at[:, own_rows(k), :],
            send_sem=f_send.at[d],
            recv_sem=f_recv.at[d],
            device_id={"chan": lax.rem(k + d, 16)},
            device_id_type=MESH,
        )

    gather_class(0, 0)
    filter_class(0)
    lane = lax.broadcasted_iota(jnp.int32, (96, 128), 1)

    for tile in range(4):
        parts = [
            f_ref[:, b, :, tile * 128 : tile * 128 + 128].reshape(96, 128).astype(F32)
            for b in range(3)
        ]
        for j in range(4):
            out = jnp.zeros((96, 128), F32)
            for b in range(3):
                moved = parts[b]
                if (b - j) % 4:
                    moved = pltpu.roll(moved, ((b - j) % 4) * 32, 1)
                out = jnp.where(lane // 32 == b, moved, out)
            f_msg[tile * 4 + j] = out.astype(BF16).reshape(3, 32, 128)

    f_all[:, own_rows(k), :] = f_msg[k]

    gather_stage(0, 2)
    gather_stage(0, 3)
    gather_class(0, 1)
    filter_class(1)
    gather_class(0, 3)
    filter_class(3)
    gather_stage(0, 4)
    gather_class(0, 2)
    filter_class(2)
    gather_stage(1, 0)
    sum_along_z(0)
    gather_stage(1, 1)
    for d in range(1, 16):
        start(f_copy(d))
    sum_along_z(1)
    sum_along_z(3)
    hand_out(0)
    gather_stage(1, 2)

    lane32 = lax.broadcasted_iota(jnp.int32, (32, cols), 1)

    def edge_copy(which, side, device):
        return pltpu.make_async_remote_copy(
            src_ref=e_out.at[which, side],
            dst_ref=e_in.at[which, side],
            send_sem=e_send.at[which, side],
            recv_sem=e_recv.at[which, side],
            device_id={"width": device},
            device_id_type=MESH,
        )

    def edges_out(which, taps):
        for h in range(2):
            e_out[which, 0, h] = taps[h][0][:, cols - 128 : cols]
            e_out[which, 1, h] = taps[h][2][:, 0:128]
        copies = [edge_copy(which, 0, right), edge_copy(which, 1, left)]
        for copy in copies:
            start(copy)
        for h in range(2):
            moved_right = jnp.where(lane32 == 0, 0.0, pltpu.roll(taps[h][0], 1, 1))
            moved_left = jnp.where(lane32 == cols - 1, 0.0, pltpu.roll(taps[h][2], cols - 1, 1))
            y_buf[which, h] = taps[h][1] + moved_right + moved_left
        return copies

    def edges_in(which, copies, out_ref):
        for copy in copies:
            copy.wait_recv()
        lane128 = lax.broadcasted_iota(jnp.int32, (32, 128), 1)
        for h in range(2):
            came = pltpu.roll(e_in[which, 0, h], 1, 1)
            y_buf[which, h, :, 0:128] += jnp.where((lane128 == 0) & (w > 0), came, 0.0)
            came = pltpu.roll(e_in[which, 1, h], 127, 1)
            y_buf[which, h, :, cols - 128 : cols] += jnp.where(
                (lane128 == 127) & (w < n_width - 1), came, 0.0
            )
            out_ref[h] = y_buf[which, h].astype(BF16)

    sums = None
    for h in range(2):
        block = f_ref[1 - h : 3 - h].reshape(192, f_ref.shape[3])
        term = jnp.dot(block, g_all[h], preferred_element_type=F32)
        sums = term if sums is None else sums + term
    taps = [[sums[h * 96 + b * 32 : h * 96 + b * 32 + 32] for b in (2, 1, 0)] for h in range(2)]
    grad_copies = edges_out(1, taps)

    sum_along_z(2)
    hand_out(1)
    hand_out(3)
    gather_stage(1, 3)
    gather_stage(1, 4)
    hand_out(2)
    relay(0)
    relay(1)
    relay(3)

    for which_dy in range(4):
        gather_class(1, which_dy)
    for d in range(1, 16):
        source = lax.rem(k + 16 - d, 16)
        pltpu.make_async_remote_copy(
            src_ref=f_msg.at[0],
            dst_ref=f_all.at[:, own_rows(source), :],
            send_sem=f_send.at[d],
            recv_sem=f_recv.at[d],
            device_id={"chan": source},
            device_id_type=MESH,
        ).wait_recv()
    depth = f_all.shape[1]
    field = x_all[...].reshape(2 * depth, cols)
    taps = []
    for h in range(2):
        block = f_all[1 - h : 3 - h].reshape(2 * depth, 128)
        sums = lax.dot_general(
            block, field, (((0,), (0,)), ((), ())), preferred_element_type=F32
        )
        taps.append([sums[b * 32 : b * 32 + 32] for b in range(3)])
    conv_copies = edges_out(0, taps)
    relay(2)
    edges_in(1, grad_copies, grad_ref)
    edges_in(0, conv_copies, conv_ref)

    for dy in (0, 1, 3, 2):
        for d in range(0 if dy in BOTH else n_z):
            source = lax.rem(across + n_width - 2 * d, n_width)
            ag_copy(dy, source, n_z + d, across).wait_recv()
    for copy in pending:
        copy.wait_send()


def finish(conv_in, grad_in, blocks, conv_ref, grad_ref, filt_ref):
    for group in range(blocks.shape[0]):
        for tap in range(9):
            filt_ref[tap, :, group * 128 : group * 128 + 128] = blocks[group, :, tap].reshape(
                filt_ref.shape[1], 128
            )
    for source, target in ((conv_in, conv_ref), (grad_in, grad_ref)):
        for h in range(2):
            target[:, h, :] = source[h]


def body(activations, filters, cotangent):
    cin_dev, rows, cols = activations.shape
    n_out = filters.shape[3]
    n_width = lax.axis_size("width")
    factor = 1.0 / math.sqrt(rows * cols * n_width)
    x = jnp.transpose(activations, (1, 0, 2))
    g = jnp.transpose(cotangent, (1, 0, 2))
    f = jnp.transpose(filters, (1, 2, 0, 3))
    vmem = pl.BlockSpec(memory_space=pltpu.VMEM)
    dma = pltpu.SemaphoreType.DMA

    def run(*refs):
        kernel(n_width, factor, *refs)

    conv, grad, filt = pl.pallas_call(
        run,
        out_shape=[
            jax.ShapeDtypeStruct((rows, cin_dev, cols), BF16),
            jax.ShapeDtypeStruct((rows, cin_dev, cols), BF16),
            jax.ShapeDtypeStruct((4, n_width, 9, 2, 128), F32),
        ],
        in_specs=[vmem] * 3,
        out_specs=[vmem] * 3,
        scratch_shapes=[
            pltpu.VMEM((rows, n_out, cols), BF16),
            pltpu.VMEM((rows, n_out, cols), BF16),
            pltpu.VMEM((3, n_out, 128), BF16),
            pltpu.VMEM((16, 3, cin_dev, 128), BF16),
            pltpu.VMEM((2, rows, cin_dev, 128), BF16),
            pltpu.VMEM((192, cols), BF16),
            pltpu.VMEM((4, n_width, 9, 2, 128), F32),
            pltpu.VMEM((4, 2, 9, 2, 128), F32),
            pltpu.VMEM((n_width // 2, 4, 2, 9, 2, 128), F32),
            pltpu.VMEM((2, 2, rows, cin_dev, 128), F32),
            pltpu.VMEM((2, 2, rows, cin_dev, 128), F32),
            pltpu.VMEM((2, rows, cin_dev, cols), F32),
            dma((2, N_MSG)),
            dma((2, N_MSG)),
            dma((16,)),
            dma((16,)),
            dma((2,)),
            dma((2,)),
            dma((4,)),
            dma((4,)),
            dma((4, n_width // 2)),
            dma((4, n_width // 2)),
            dma((4, n_width)),
            dma((4, n_width)),
            dma((2, 2)),
            dma((2, 2)),
        ],
        compiler_params=pltpu.CompilerParams(
            collective_id=0, has_side_effects=True, vmem_limit_bytes=20 * 1024 * 1024
        ),
        name="conv_all",
    )(x, g, f)
    conv, grad, filt = pl.pallas_call(
        finish,
        out_shape=[
            jax.ShapeDtypeStruct((cin_dev, rows, cols), BF16),
            jax.ShapeDtypeStruct((cin_dev, rows, cols), BF16),
            jax.ShapeDtypeStruct((9, cin_dev, n_out), F32),
        ],
        in_specs=[vmem] * 3,
        out_specs=[vmem] * 3,
        compiler_params=pltpu.CompilerParams(vmem_limit_bytes=8 * 1024 * 1024),
        name="finish",
    )(conv, grad, filt)
    filt = jnp.transpose(filt.reshape(3, 3, cin_dev, n_out), (2, 0, 1, 3))
    return conv, grad, filt


def solution(mesh):
    in_specs = (P("chan", None, "width"), P("chan", None, None, None), P("chan", None, "width"))
    out_specs = (P("chan", None, "width"), P("chan", None, "width"), P("chan", None, None, None))
    return jax.shard_map(body, mesh=mesh, in_specs=in_specs, out_specs=out_specs, check_vma=False)
```
